32 devices in a mesh: dp: 8 (over y, x, core), span: 4 (over z).
Axes of the slice: x: 2, y: 2, z: 4, core: 2. Of those that a mesh axis runs over, the one named last changes fastest.
Arguments:
- features: bfloat16 [8, 1024, 1024], P('dp', 'span'), may hold values from -6 to 6
- lengths: int32 [8], P('dp'), may hold values from 256 to 1024, as said below
- labels: int32 [8, 1024], P('dp', 'span'), may hold values from 0 to 4
- w_first: bfloat16 [1024, 1024], replicated, may hold values from -0.1875 to 0.1875
- b_first: float32 [1024], replicated, may hold values from -3 to 3
- w_second: bfloat16 [1024, 256], replicated, may hold values from -0.375 to 0.375
Outputs:
- loss: float32 [], replicated
- grad_first: float32 [1024, 1024], replicated
- grad_bias: float32 [1024], replicated
- grad_second: float32 [1024, 256], replicated
The draws below stay inside these ranges and needn't reach their ends.
Inputs may be any that keep to these rules, and one draw needn't show every extreme that they name: `lengths`: every list has 256 or more real candidates, and some list has exactly 1024.
All inputs are finite; a program needn't handle non-finite values.
Results may differ from the reference program's by a relative error of at most 0.004.
Values may be sent and summed in bfloat16 or wider, within the bound.
A program may use at most 64 MiB of HBM per device.

```python
import math
import jax
import jax.numpy as jnp
from jax import lax

D_IN = 1024
HID = 1024
EMB = 128
CAND_DEV = 256
LIST = 1024
LISTS = 8


def draw_lengths(key, part):
    key_draw, key_chosen = jax.random.split(key)
    sampled = jax.random.randint(key_draw, (LISTS,), CAND_DEV, LIST + 1)
    chosen = jax.random.randint(key_chosen, (), 0, LISTS)
    return jnp.where(jnp.arange(LISTS) == chosen, LIST, sampled).astype(jnp.int32)


def touch_ends(drawn, rng, least, high):
    longest = drawn.shape.index(max(drawn.shape))
    spots = []
    for shift in (0, 1):
        where = [jax.random.randint(jax.random.fold_in(rng, axis), (), 0, length) for axis, length in enumerate(drawn.shape)]
        where[longest] = (where[longest] + shift) % drawn.shape[longest]
        spots.append(tuple(where))
    return drawn.at[spots[0]].set(least).at[spots[1]].set(high)


def block_levels(rng, shape, cuts, smallest, top_value):
    def one(axis_at, parts):
        steps = jax.random.uniform(jax.random.fold_in(jax.random.fold_in(rng, 6), axis_at), (parts,), jnp.float32, smallest / len(cuts), top_value / len(cuts))
        return jnp.repeat(jnp.exp(steps), shape[axis_at] // parts).reshape((-1,) + (1,) * (len(shape) - axis_at - 1))

    loudness = one(*cuts[0])
    for cut in cuts[1:]:
        loudness = loudness * one(*cut)
    return loudness


def bell_draw(stream_key, dims, scale, bound, cuts=(), held_as=jnp.bfloat16):
    factor_of = block_levels(stream_key, dims, cuts, -0.22, 0.18) if cuts else 1.0
    values = jax.random.normal(stream_key, dims, jnp.float32) * scale * factor_of
    return jnp.minimum(jnp.maximum(values, -bound), bound).astype(held_as)


def setup_inputs(seed: int = 0) -> dict:
    key_list = jax.random.split(jax.random.key(seed), 7)
    features = bell_draw(key_list[0], (LISTS, LIST, D_IN), 1.0, 6.0, ((0, 8), (1, 4)))
    lengths = draw_lengths(jax.random.fold_in(key_list[6], 71), 0)
    labels = touch_ends(jax.random.randint(key_list[2], (LISTS, LIST), 0, 5), jax.random.fold_in(key_list[2], 1), 0, 4).astype(jnp.int32)
    w_first = bell_draw(key_list[3], (D_IN, HID), D_IN ** -0.5, 0.1875)
    b_first = bell_draw(key_list[4], (HID,), 0.5, 3.0, (), jnp.float32)
    w_second = bell_draw(key_list[5], (HID, 2 * EMB), (HID // 4) ** -0.5, 0.375)
    return {"features": features, "lengths": lengths, "labels": labels, "w_first": w_first, "b_first": b_first, "w_second": w_second}


gain_values = (0.0, 1.0, 3.0, 7.0, 15.0)
log_two = math.log(2.0)

def level_onehot(labels):
    return (labels[..., None] == jnp.arange(5, dtype=jnp.int32)).astype(jnp.float32)

def ideal_gain(level_counts, list_len):
    levels = jnp.arange(5, dtype=jnp.int32)
    above_mask = (levels[:, None] > levels[None, :]).astype(jnp.float32)
    starts = lax.optimization_barrier(jnp.sum(level_counts[:, None] * above_mask, axis=0))
    finish = starts + level_counts
    places = jnp.arange(1, list_len + 1, dtype=jnp.int32).astype(jnp.float32)
    discount = log_two / jnp.log1p(places)
    inside = (places[None, :] > starts[:, None]) & (places[None, :] <= finish[:, None])
    per_level = lax.optimization_barrier(jnp.sum(jnp.where(inside, discount[None, :], 0.0), axis=1))
    return jnp.maximum(jnp.sum(per_level * jnp.asarray(gain_values, jnp.float32)), 1.0)

def pair_logits(row_emb, key_rows, pair_scale):
    return jnp.einsum('ik,jk->ij', row_emb.astype(jnp.float32), key_rows.astype(jnp.float32), precision=lax.Precision.HIGHEST) * pair_scale

def reference(features, lengths, labels, w_first, b_first, w_second):
    list_count = labels.shape[0]
    list_len = labels.shape[1]
    half_width = w_second.shape[1] // 2
    pair_scale = 1.0 / math.sqrt(half_width)

    def per_list(list_args):
        list_feats, length, list_labels = list_args
        in_list = (jnp.arange(list_len, dtype=jnp.int32) < length).astype(jnp.float32)
        onehot = level_onehot(list_labels) * in_list[:, None]
        gain_row = lax.optimization_barrier(jnp.sum(onehot * jnp.asarray(gain_values, jnp.float32)[None, :], axis=1))
        ideal = ideal_gain(lax.optimization_barrier(jnp.sum(onehot, axis=0)), list_len)
        pre_act = jnp.dot(list_feats, w_first, preferred_element_type=jnp.float32) + b_first[None, :]
        hidden = jnp.maximum(pre_act, 0.0).astype(jnp.bfloat16)
        row_emb = jnp.dot(hidden, w_second, preferred_element_type=jnp.float32).astype(jnp.bfloat16)
        key_rows = jnp.concatenate([row_emb[:, half_width:], -row_emb[:, :half_width]], axis=1)
        emb_blocks = row_emb.reshape(list_len // CAND_DEV, CAND_DEV, 2 * half_width)

        def rank_rows(block_emb):
            logits = pair_logits(block_emb, key_rows, pair_scale)
            return lax.optimization_barrier(jnp.sum(jax.nn.sigmoid(-logits) * in_list[None, :], axis=1))
        soft_rank = 0.5 + lax.map(rank_rows, emb_blocks).reshape(list_len)
        log_rank = jnp.log1p(soft_rank)
        approx_dcg = jnp.sum(gain_row * log_two / log_rank)
        loss_term = (1.0 - approx_dcg / ideal) / list_count
        row_weight = gain_row / (ideal * list_count) * log_two / ((1.0 + soft_rank) * log_rank * log_rank)

        def grad_rows_block(block_args):
            block_emb, block_weight, block_live = block_args
            logits = pair_logits(block_emb, key_rows, pair_scale)
            probab = jax.nn.sigmoid(logits)
            pair_grad = probab * (1.0 - probab) * (block_live[:, None] * row_weight[None, :] - block_weight[:, None] * in_list[None, :])
            return jnp.dot(pair_grad.astype(jnp.bfloat16), key_rows, preferred_element_type=jnp.float32) * pair_scale
        grad_sum = lax.map(grad_rows_block, (emb_blocks, row_weight.reshape(-1, CAND_DEV), in_list.reshape(-1, CAND_DEV)))
        grad_emb = grad_sum.reshape(list_len, 2 * half_width).astype(jnp.bfloat16)
        grad_second = jnp.einsum('ch,ce->he', hidden.astype(jnp.float32), grad_emb.astype(jnp.float32), precision=lax.Precision.HIGHEST)
        back_hidden = jnp.einsum('ce,he->ch', grad_emb.astype(jnp.float32), w_second.astype(jnp.float32), precision=lax.Precision.HIGHEST)
        grad_pre = jnp.where(pre_act > 0.0, back_hidden, 0.0).astype(jnp.bfloat16)
        grad_bias = lax.optimization_barrier(jnp.sum(grad_pre.astype(jnp.float32), axis=0))
        grad_first = jnp.einsum('cd,ch->dh', list_feats.astype(jnp.float32), grad_pre.astype(jnp.float32), precision=lax.Precision.HIGHEST)
        return (grad_first, grad_bias, grad_second, loss_term)
    results = lax.map(per_list, (features, lengths, labels))
    return (jnp.sum(results[3]), lax.optimization_barrier(jnp.sum(results[0], axis=0)), lax.optimization_barrier(jnp.sum(results[1], axis=0)), lax.optimization_barrier(jnp.sum(results[2], axis=0)))
```

```python
import math

import jax
import jax.numpy as jnp
from jax import lax
from jax.experimental import pallas as pl
from jax.experimental.pallas import tpu as pltpu
from jax.sharding import PartitionSpec as P

gain_values = (0.0, 1.0, 3.0, 7.0, 15.0)
log_two = math.log(2.0)


def greet_peers(place, chips, spans):
    core, chip, span = place
    barrier = pltpu.get_barrier_semaphore()
    peers = [{"dp": 2 * chip + 1 - core, "span": span}]
    peers += [{"dp": 2 * lax.rem(chip + k, chips) + core, "span": span} for k in range(1, chips)]
    peers += [{"dp": 2 * chip + core, "span": lax.rem(span + k, spans)} for k in range(1, spans)]
    for peer in peers:
        pl.semaphore_signal(barrier, inc=1, device_id=peer, device_id_type=pl.DeviceIdType.MESH)
    return lambda: pl.semaphore_wait(barrier, len(peers))


def rows_at(start, size):
    return pl.ds(pl.multiple_of(start, size), size)


def owners_of(rows, chips, spans):
    block = rows // 2 // chips
    return min(spans, block // 16)


class Reducer:
    def __init__(self, place, chips, spans, grads, result, small, small_out, scratch):
        self.core, self.chip, self.span = place
        self.chips, self.spans = chips, spans
        self.grads, self.result = grads, result
        self.small, self.small_out = small, small_out
        (
            self.pair_in, self.half_sum, self.half_buf, self.chip_in,
            self.block_sum, self.block_buf, self.span_in,
            self.small_pair, self.small_chip, self.small_span,
            self.pair_s, self.pair_r, self.chip_s, self.chip_r, self.span_s, self.span_r,
            self.small_s, self.small_r,
        ) = scratch
        self.half = self.pair_in.shape[1]
        self.block = self.half // chips
        self.part = self.span_in.shape[2]
        self.owners = self.block // self.part
        self.copies = {}

    def copy(self, key, src, dst, send, recv, dp=None, span=None):
        peer = {
            "dp": 2 * self.chip + self.core if dp is None else dp,
            "span": self.span if span is None else span,
        }
        made = pltpu.make_async_remote_copy(
            src_ref=src, dst_ref=dst, send_sem=send, recv_sem=recv,
            device_id=peer, device_id_type=pl.DeviceIdType.MESH,
        )
        made.start()
        self.copies.setdefault(key, []).append(made)

    def settle(self, key):
        for made in self.copies.pop(key, []):
            made.wait()

    def partner(self):
        return 2 * self.chip + 1 - self.core

    def other_chip(self, k):
        return 2 * lax.rem(self.chip + k, self.chips) + self.core

    def pair_out(self, p):
        away = self.grads.at[p, rows_at((1 - self.core) * self.half, self.half)]
        self.copy(("pair", p), away, self.pair_in.at[p], self.pair_s.at[0, p], self.pair_r.at[0, p], dp=self.partner())

    def chip_out(self, p):
        self.settle(("pair", p))
        own = self.grads[p, rows_at(self.core * self.half, self.half), :]
        total = own + self.pair_in[p]
        self.half_sum[p] = total
        self.half_buf[p] = total.astype(jnp.bfloat16)
        for k in range(1, self.chips):
            rows = rows_at(lax.rem(self.chip + k, self.chips) * self.block, self.block)
            self.copy(("chip", p), self.half_buf.at[p, rows], self.chip_in.at[p, k - 1], self.chip_s.at[0, p, k - 1], self.chip_r.at[0, p, k - 1], dp=self.other_chip(k))

    def span_out(self, p):
        self.settle(("chip", p))
        total = self.half_sum[p, rows_at(self.chip * self.block, self.block)]
        for k in range(1, self.chips):
            total = total + self.chip_in[p, k - 1].astype(jnp.float32)
        self.block_sum[p] = total
        self.block_buf[p] = total.astype(jnp.bfloat16)
        for k in range(1, self.spans):
            to = lax.rem(self.span + k, self.spans)
            rows = rows_at(lax.rem(to, self.owners) * self.part, self.part)
            self.copy(("span", p), self.block_buf.at[p, rows], self.span_in.at[p, k - 1], self.span_s.at[0, p, k - 1], self.span_r.at[0, p, k - 1], span=to)

    def span_back(self, p):
        self.settle(("span", p))
        mine = lax.rem(self.span, self.owners)
        rows = rows_at(mine * self.part, self.part)
        if self.owners == self.spans:
            total = self.block_sum[p, rows]
        else:
            total = self.block_buf[p, rows].astype(jnp.float32)
        for k in range(1, self.spans):
            total = total + self.span_in[p, k - 1].astype(jnp.float32)
        start = self.core * self.half + self.chip * self.block + mine * self.part
        place = self.result(p, rows_at(start, self.part))
        place[...] = total.astype(jnp.bfloat16)
        for k in range(1, self.owners):
            to = self.span - mine + lax.rem(mine + k, self.owners)
            self.copy(("span_back", p), place, place, self.span_s.at[1, p, k - 1], self.span_r.at[1, p, k - 1], span=to)

    def chip_back(self, p):
        self.settle(("span_back", p))
        place = self.result(p, rows_at(self.core * self.half + self.chip * self.block, self.block))
        for k in range(1, self.chips):
            self.copy(("chip_back", p), place, place, self.chip_s.at[1, p, k - 1], self.chip_r.at[1, p, k - 1], dp=self.other_chip(k))

    def pair_back(self, p):
        self.settle(("chip_back", p))
        place = self.result(p, rows_at(self.core * self.half, self.half))
        self.copy(("pair_back", p), place, place, self.pair_s.at[1, p], self.pair_r.at[1, p], dp=self.partner())

    def small_first(self):
        self.small_pair[self.core] = self.small()
        place = self.small_pair.at[self.core]
        self.copy("small0", place, place, self.small_s.at[0], self.small_r.at[0], dp=self.partner())

    def small_second(self):
        self.settle("small0")
        self.small_chip[self.chip] = self.small_pair[0] + self.small_pair[1]
        place = self.small_chip.at[self.chip]
        for k in range(1, self.chips):
            self.copy("small1", place, place, self.small_s.at[k], self.small_r.at[k], dp=self.other_chip(k))

    def small_third(self):
        self.settle("small1")
        total = self.small_chip[0]
        for k in range(1, self.chips):
            total = total + self.small_chip[k]
        self.small_span[self.span] = total
        place = self.small_span.at[self.span]
        for k in range(1, self.spans):
            at = self.chips + k - 1
            self.copy("small2", place, place, self.small_s.at[at], self.small_r.at[at], span=lax.rem(self.span + k, self.spans))

    def small_last(self):
        self.settle("small2")
        total = self.small_span[0]
        for k in range(1, self.spans):
            total = total + self.small_span[k]
        self.small_out[...] = total


def reducer_scratch(pieces, rows, width, chips, spans, small_shape):
    half = rows // 2
    block = half // chips
    part = block // owners_of(rows, chips, spans)
    vmem, dma = pltpu.VMEM, pltpu.SemaphoreType.DMA
    return [
        vmem((pieces, half, width), jnp.float32),
        vmem((pieces, half, width), jnp.float32),
        vmem((pieces, half, width), jnp.bfloat16),
        vmem((pieces, chips - 1, block, width), jnp.bfloat16),
        vmem((pieces, block, width), jnp.float32),
        vmem((pieces, block, width), jnp.bfloat16),
        vmem((pieces, spans - 1, part, width), jnp.bfloat16),
        vmem((2,) + small_shape, jnp.float32),
        vmem((chips,) + small_shape, jnp.float32),
        vmem((spans,) + small_shape, jnp.float32),
        dma((2, pieces)), dma((2, pieces)),
        dma((2, pieces, chips - 1)), dma((2, pieces, chips - 1)),
        dma((2, pieces, spans - 1)), dma((2, pieces, spans - 1)),
        dma((chips + spans,)), dma((chips + spans,)),
    ]


def finish_reduce(red, pieces):
    stages = (red.span_out, red.span_back, red.chip_back, red.pair_back, lambda p: red.settle(("pair_back", p)))
    order = sorted((p + lag, n, p) for p in range(pieces) for n, lag in enumerate((0, 2.2, 4.3, 6.5, 9.0)))
    smalls = {0: red.small_second, 3: red.small_third, 8: red.small_last}
    for at, (_, n, p) in enumerate(order):
        stages[n](p)
        if at in smalls:
            smalls[at]()


def write_kernel(first, second, small, first_out, second_out, bias_out, loss_out, first_buf, second_buf, sem):
    parts = first_buf.shape[0]
    rows = first_buf.shape[1]
    copies = [pltpu.make_async_copy(second_buf, second_out, sem.at[parts])]
    second_buf[...] = second[...].astype(jnp.float32)
    copies[0].start()
    for n in range(parts):
        at = pl.ds(n * rows, rows)
        first_buf[n] = first[at, :].astype(jnp.float32)
        copies.append(pltpu.make_async_copy(first_buf.at[n], first_out.at[at], sem.at[n]))
        copies[-1].start()
    hid = bias_out.shape[1]
    bias_out[...] = small[:, pl.ds(0, hid)]
    loss_out[...] = small[:, pl.ds(hid, 1)]
    for copy in copies:
        copy.wait()


def dot(lhs, rhs, dims):
    return lax.dot_general(lhs, rhs, (dims, ((), ())), preferred_element_type=jnp.float32)


def ideal_gain(counts, list_len):
    places = (1 + lax.broadcasted_iota(jnp.int32, (1, list_len), 1)).astype(jnp.float32)
    discount = log_two / jnp.log(1.0 + places)
    total = jnp.zeros((1, 1), jnp.float32)
    start = jnp.zeros((1, 1), jnp.float32)
    for level in reversed(range(len(gain_values))):
        finish = start + counts[level : level + 1, 0:1]
        inside = (places > start) & (places <= finish)
        total = total + gain_values[level] * jnp.sum(jnp.where(inside, discount, 0.0), axis=1, keepdims=True)
        start = finish
    return jnp.maximum(total, 1.0)


def step_kernel(
    chips, spans, lengths, labels_hbm, features_hbm, w_first_hbm, b_first_hbm, w_second_hbm,
    first_out, second_out, small_out,
    feats, w_first, w_second, feats_t, hidden_t, pre, hidden, emb, keys, slopes, weights, counts, grads, small,
    labels, b_first, load_sem, key_s, key_r, weight_s, weight_r, count_s, count_r, *scratch,
):
    dp, span = lax.axis_index("dp"), lax.axis_index("span")
    place = (lax.rem(dp, 2), dp // 2, span)
    rows = feats.shape[0]
    width = w_second.shape[1]
    hid = w_first.shape[1]
    half_width = width // 2
    pair_scale = 1.0 / math.sqrt(half_width)
    pieces = 1 + hid // width
    list_count, list_len = 2 * chips, rows * spans
    loads = [
        pltpu.make_async_copy(src, dst, load_sem.at[n])
        for n, (src, dst) in enumerate(
            (
                (features_hbm.at[0], feats), (w_first_hbm, w_first), (w_second_hbm, w_second),
                (labels_hbm, labels), (b_first_hbm, b_first),
            )
        )
    ]
    for load in loads:
        load.start()
    enter = greet_peers(place, chips, spans)

    def to_peers(make_src, dst, send, recv):
        made = []
        for k in range(1, spans):
            copy = pltpu.make_async_remote_copy(
                src_ref=make_src, dst_ref=dst.at[k], send_sem=send.at[k - 1], recv_sem=recv.at[k - 1],
                device_id={"dp": dp, "span": lax.rem(span + k, spans)}, device_id_type=pl.DeviceIdType.MESH,
            )
            copy.start()
            made.append(copy)
        return made

    for load in loads[3:]:
        load.wait()
    length = lengths[0]
    slots = lax.broadcasted_iota(jnp.int32, (1, rows), 1)

    def live_row(k):
        owner = lax.rem(span - k + spans, spans)
        return (owner * rows + slots < length).astype(jnp.float32)

    own_live = live_row(0)
    live_col = (span * rows + lax.broadcasted_iota(jnp.int32, (rows, 1), 0) < length).astype(jnp.float32)
    eye = lax.broadcasted_iota(jnp.int32, (rows, rows), 0) == lax.broadcasted_iota(jnp.int32, (rows, rows), 1)
    label_row = labels[...].astype(jnp.float32)
    label_col = jnp.sum(jnp.where(eye, label_row, 0.0), axis=1, keepdims=True)
    gain = jnp.zeros((rows, 1), jnp.float32)
    for level, value in enumerate(gain_values):
        gain = gain + jnp.where(label_col == level, value, 0.0)
    gain = gain * live_col
    levels = lax.broadcasted_iota(jnp.int32, (8, rows), 0).astype(jnp.float32)
    level_counts = jnp.sum(jnp.where(levels == label_row, own_live, 0.0), axis=1, keepdims=True)
    counts[0] = jnp.broadcast_to(level_counts, counts.shape[1:])

    loads[0].wait()
    loads[1].wait()
    for p in range(pieces - 1):
        cols = pl.ds(p * width, width)
        pre_act = dot(feats[...], w_first[:, cols], ((1,), (0,))) + b_first[:, cols]
        pre[:, cols] = pre_act
        hidden[:, cols] = jnp.maximum(pre_act, 0.0).astype(jnp.bfloat16)
    loads[2].wait()
    row_emb = dot(hidden[...], w_second[...], ((1,), (0,))).astype(jnp.bfloat16)
    emb[...] = row_emb
    keys[0] = jnp.concatenate([row_emb[:, half_width:], -row_emb[:, :half_width]], axis=1)
    enter()
    key_copies = to_peers(keys.at[0], keys, key_s, key_r)
    count_copies = to_peers(counts.at[0], counts, count_s, count_r)
    feats_t[...] = feats[...].T
    hidden_t[...] = hidden[...].T

    rank = jnp.full((rows, 1), 0.5, jnp.float32)
    for k in range(spans):
        if k:
            key_copies[k - 1].wait()
        logits = dot(emb[...], keys[k], ((1,), (1,))) * pair_scale
        below = jax.nn.sigmoid(-logits)
        slopes[k] = below * (1.0 - below)
        rank = rank + jnp.sum(below * live_row(k), axis=1, keepdims=True)
    for copy in count_copies:
        copy.wait()
    all_counts = counts[0]
    for k in range(1, spans):
        all_counts = all_counts + counts[k]
    ideal = ideal_gain(all_counts, list_len)
    log_rank = jnp.log(1.0 + rank)
    weight = gain / (ideal * list_count) * log_two / ((1.0 + rank) * log_rank * log_rank)
    weights[0] = jnp.broadcast_to(jnp.sum(jnp.where(eye, weight, 0.0), axis=0, keepdims=True), weights.shape[1:])
    weight_copies = to_peers(weights.at[0], weights, weight_s, weight_r)
    dcg = jnp.sum(gain * log_two / log_rank, axis=0, keepdims=True)
    loss_part = (1.0 / spans - dcg / ideal) / list_count
    small[:, pl.ds(hid, 128)] = jnp.broadcast_to(loss_part, (1, 128))

    total = jnp.zeros((rows, width), jnp.float32)
    for k in range(spans):
        if k:
            weight_copies[k - 1].wait()
        pair_grad = slopes[k] * (live_col * weights[k, 0:1, :] - weight * live_row(k))
        total = total + dot(pair_grad.astype(jnp.bfloat16), keys[k], ((1,), (0,)))
    grad_emb = (total * pair_scale).astype(jnp.bfloat16)

    def result(p, at):
        return second_out.at[at] if p == 0 else first_out.at[at, pl.ds((p - 1) * width, width)]

    red = Reducer(place, chips, spans, grads, result, lambda: small[...], small_out, scratch)
    grads[0] = dot(hidden_t[...], grad_emb, ((1,), (0,)))
    red.pair_out(0)
    for p in range(1, pieces):
        cols = pl.ds((p - 1) * width, width)
        back = dot(grad_emb, w_second[cols, :], ((1,), (1,)))
        grad_pre = jnp.where(pre[:, cols] > 0.0, back, 0.0).astype(jnp.bfloat16)
        small[:, cols] = jnp.sum(grad_pre.astype(jnp.float32), axis=0, keepdims=True)
        grads[p] = dot(feats_t[...], grad_pre, ((1,), (0,)))
        red.pair_out(p)
        red.chip_out(p - 1)
    red.small_first()
    red.chip_out(pieces - 1)
    finish_reduce(red, pieces)


def shards(features, lengths, labels, w_first, b_first, w_second):
    chips, spans = lax.axis_size("dp") // 2, lax.axis_size("span")
    rows, depth = features.shape[1:]
    hid, width = w_second.shape
    pieces = 1 + hid // width
    small_shape = (1, hid + 128)
    vmem, dma = pltpu.VMEM, pltpu.SemaphoreType.DMA
    in_vmem = pl.BlockSpec(memory_space=pltpu.VMEM)
    in_place = pl.BlockSpec(memory_space=pl.ANY)
    in_hbm = pl.BlockSpec(memory_space=pltpu.HBM)
    first_sum, second_sum, small_sum = pl.pallas_call(
        lambda *refs: step_kernel(chips, spans, *refs),
        name="rank_step",
        out_shape=(
            jax.ShapeDtypeStruct((depth, hid), jnp.bfloat16),
            jax.ShapeDtypeStruct((hid, width), jnp.bfloat16),
            jax.ShapeDtypeStruct(small_shape, jnp.float32),
        ),
        in_specs=[pl.BlockSpec(memory_space=pltpu.SMEM)] + [in_hbm] * 5,
        out_specs=(in_vmem,) * 3,
        scratch_shapes=[
            vmem((rows, depth), jnp.bfloat16),
            vmem((depth, hid), jnp.bfloat16),
            vmem((hid, width), jnp.bfloat16),
            vmem((depth, rows), jnp.bfloat16),
            vmem((hid, rows), jnp.bfloat16),
            vmem((rows, hid), jnp.float32),
            vmem((rows, hid), jnp.bfloat16),
            vmem((rows, width), jnp.bfloat16),
            vmem((spans, rows, width), jnp.bfloat16),
            vmem((spans, rows, rows), jnp.float32),
            vmem((spans, 8, rows), jnp.float32),
            vmem((spans, 8, 128), jnp.float32),
            vmem((pieces, hid, width), jnp.float32),
            vmem(small_shape, jnp.float32),
            vmem((1, rows), jnp.int32), vmem((1, hid), jnp.float32),
            dma((5,)),
            dma((spans - 1,)), dma((spans - 1,)), dma((spans - 1,)),
            dma((spans - 1,)), dma((spans - 1,)), dma((spans - 1,)),
        ]
        + reducer_scratch(pieces, hid, width, chips, spans, small_shape),
        compiler_params=pltpu.CompilerParams(collective_id=0, has_side_effects=True, vmem_limit_bytes=40 << 20),
    )(lengths, *(pltpu.with_memory_space_constraint(x, pltpu.HBM) for x in (labels, features, w_first, b_first.reshape(1, -1), w_second)))
    parts = 4
    first, second, bias, loss = pl.pallas_call(
        write_kernel,
        name="write_out",
        out_shape=(
            jax.ShapeDtypeStruct((depth, hid), jnp.float32),
            jax.ShapeDtypeStruct((hid, width), jnp.float32),
            jax.ShapeDtypeStruct((1, hid), jnp.float32),
            jax.ShapeDtypeStruct((1, 1), jnp.float32),
        ),
        in_specs=[in_vmem] * 3,
        out_specs=(in_place, in_place, in_vmem, in_vmem),
        scratch_shapes=[
            vmem((parts, depth // parts, hid), jnp.float32),
            vmem((hid, width), jnp.float32),
            dma((parts + 1,)),
        ],
        compiler_params=pltpu.CompilerParams(vmem_limit_bytes=16 << 20),
    )(first_sum, second_sum, small_sum)
    return loss[0, 0], first, bias[0], second


def solution(mesh):
    placed = (P("dp", "span", None), P("dp"), P("dp", "span"), P(), P(), P())
    return jax.shard_map(
        shards, mesh=mesh, in_specs=placed, out_specs=(P(), P(), P(), P()), check_vma=False
    )
```

```python
import math

import jax
import jax.numpy as jnp
from jax import lax
from jax.experimental import pallas as pl
from jax.experimental.pallas import tpu as pltpu
from jax.sharding import PartitionSpec as P

gain_values = (0.0, 1.0, 3.0, 7.0, 15.0)
log_two = math.log(2.0)


def greet_peers(place, chips, spans):
    core, chip, span = place
    barrier = pltpu.get_barrier_semaphore()
    peers = [{"dp": 2 * chip + 1 - core, "span": span}]
    peers += [{"dp": 2 * lax.rem(chip + k, chips) + core, "span": span} for k in range(1, chips)]
    peers += [{"dp": 2 * chip + core, "span": lax.rem(span + k, spans)} for k in range(1, spans)]
    for peer in peers:
        pl.semaphore_signal(barrier, inc=1, device_id=peer, device_id_type=pl.DeviceIdType.MESH)
    return lambda: pl.semaphore_wait(barrier, len(peers))


def rows_at(start, size):
    return pl.ds(pl.multiple_of(start, size), size)


def owners_of(rows, chips, spans):
    return min(spans, rows // chips // 16)


class Reducer:
    def __init__(self, place, chips, spans, pieces, compute, result, scratch):
        self.core, self.chip, self.span = place
        self.chips, self.spans = chips, spans
        self.compute, self.result = compute, result
        (
            self.full_sum, self.chip_buf, self.chip_in, self.block_sum, self.block_buf, self.span_in,
            self.small_chip, self.small_span, self.small_pair,
            self.pair_s, self.pair_r, self.chip_s, self.chip_r, self.span_s, self.span_r,
            self.small_s, self.small_r,
        ) = scratch
        self.rows = self.chip_buf.shape[1]
        self.block = self.chip_in.shape[2]
        self.part = self.span_in.shape[2]
        self.owners = self.block // self.part
        self.copies = {}

    def copy(self, key, src, dst, send, recv, dp=None, span=None):
        peer = {
            "dp": 2 * self.chip + self.core if dp is None else dp,
            "span": self.span if span is None else span,
        }
        made = pltpu.make_async_remote_copy(
            src_ref=src, dst_ref=dst, send_sem=send, recv_sem=recv,
            device_id=peer, device_id_type=pl.DeviceIdType.MESH,
        )
        made.start()
        self.copies.setdefault(key, []).append(made)

    def settle(self, key):
        for made in self.copies.pop(key, []):
            made.wait()

    def partner(self):
        return 2 * self.chip + 1 - self.core

    def other_chip(self, k):
        return 2 * lax.rem(self.chip + k, self.chips) + self.core

    def chip_out(self, p):
        total = self.compute(p)
        self.chip_buf[p] = total.astype(jnp.bfloat16)
        self.full_sum[p] = total
        for k in range(1, self.chips):
            rows = rows_at(lax.rem(self.chip + k, self.chips) * self.block, self.block)
            self.copy(("chip", p), self.chip_buf.at[p, rows], self.chip_in.at[p, k - 1], self.chip_s.at[0, p, k - 1], self.chip_r.at[0, p, k - 1], dp=self.other_chip(k))

    def span_out(self, p):
        self.settle(("chip", p))
        total = self.full_sum[p, rows_at(self.chip * self.block, self.block)]
        for k in range(1, self.chips):
            total = total + self.chip_in[p, k - 1].astype(jnp.float32)
        self.block_sum[p] = total
        self.block_buf[p] = total.astype(jnp.bfloat16)
        for k in range(1, self.spans):
            to = lax.rem(self.span + k, self.spans)
            rows = rows_at(lax.rem(to, self.owners) * self.part, self.part)
            self.copy(("span", p), self.block_buf.at[p, rows], self.span_in.at[p, k - 1], self.span_s.at[0, p, k - 1], self.span_r.at[0, p, k - 1], span=to)

    def span_back(self, p):
        self.settle(("span", p))
        mine = lax.rem(self.span, self.owners)
        rows = rows_at(mine * self.part, self.part)
        if self.owners == self.spans:
            total = self.block_sum[p, rows]
        else:
            total = self.block_buf[p, rows].astype(jnp.float32)
        for k in range(1, self.spans):
            total = total + self.span_in[p, k - 1].astype(jnp.float32)
        place = self.result(p, self.core, self.chip * self.block + mine * self.part, self.part)
        place[...] = total.astype(jnp.bfloat16)
        for k in range(1, self.owners):
            to = self.span - mine + lax.rem(mine + k, self.owners)
            self.copy(("span_back", p), place, place, self.span_s.at[1, p, k - 1], self.span_r.at[1, p, k - 1], span=to)

    def chip_back(self, p):
        self.settle(("span_back", p))
        place = self.result(p, self.core, self.chip * self.block, self.block)
        for k in range(1, self.chips):
            self.copy(("chip_back", p), place, place, self.chip_s.at[1, p, k - 1], self.chip_r.at[1, p, k - 1], dp=self.other_chip(k))

    def pair_back(self, p):
        self.settle(("chip_back", p))
        place = self.result(p, self.core, 0, self.rows)
        self.copy(("pair_back", p), place, place, self.pair_s.at[p], self.pair_r.at[p], dp=self.partner())

    def last(self, p):
        self.settle(("pair_back", p))

    def small_first(self, values):
        self.small_chip[self.chip] = values
        place = self.small_chip.at[self.chip]
        for k in range(1, self.chips):
            self.copy("small0", place, place, self.small_s.at[k - 1], self.small_r.at[k - 1], dp=self.other_chip(k))

    def small_second(self):
        self.settle("small0")
        total = self.small_chip[0]
        for k in range(1, self.chips):
            total = total + self.small_chip[k]
        self.small_span[self.span] = total
        place = self.small_span.at[self.span]
        for k in range(1, self.spans):
            at = self.chips + k - 2
            self.copy("small1", place, place, self.small_s.at[at], self.small_r.at[at], span=lax.rem(self.span + k, self.spans))

    def small_third(self):
        self.settle("small1")
        total = self.small_span[0]
        for k in range(1, self.spans):
            total = total + self.small_span[k]
        self.small_pair[self.core] = total
        place = self.small_pair.at[self.core]
        at = self.chips + self.spans - 2
        self.copy("small2", place, place, self.small_s.at[at], self.small_r.at[at], dp=self.partner())

    def small_last(self, out):
        self.settle("small2")
        half = self.small_pair.shape[2] - 128
        for c in range(2):
            out[:, pl.ds(c * half, half)] = self.small_pair[c, :, pl.ds(0, half)]
        out[:, pl.ds(2 * half, 128)] = self.small_pair[0, :, pl.ds(half, 128)] + self.small_pair[1, :, pl.ds(half, 128)]


def reducer_scratch(pieces, rows, width, chips, spans, small_width):
    block = rows // chips
    part = block // owners_of(rows, chips, spans)
    vmem, dma = pltpu.VMEM, pltpu.SemaphoreType.DMA
    return [
        vmem((pieces, rows, width), jnp.float32),
        vmem((pieces, rows, width), jnp.bfloat16),
        vmem((pieces, chips - 1, block, width), jnp.bfloat16),
        vmem((pieces, block, width), jnp.float32),
        vmem((pieces, block, width), jnp.bfloat16),
        vmem((pieces, spans - 1, part, width), jnp.bfloat16),
        vmem((chips, 1, small_width), jnp.float32),
        vmem((spans, 1, small_width), jnp.float32),
        vmem((2, 1, small_width), jnp.float32),
        dma((pieces,)), dma((pieces,)),
        dma((2, pieces, chips - 1)), dma((2, pieces, chips - 1)),
        dma((2, pieces, spans - 1)), dma((2, pieces, spans - 1)),
        dma((chips + spans - 1,)), dma((chips + spans - 1,)),
    ]


def finish_reduce(red, pieces, small_out):
    stages = (red.span_out, red.span_back, red.chip_back, red.pair_back, red.last)
    gap = 12.8 / pieces
    lags = (0, 4.2, 8.4, 12.6, 16.8)
    order = sorted((p * gap + lag, n, p) for p in range(pieces) for n, lag in enumerate(lags))
    smalls = [red.small_second, red.small_third, lambda: red.small_last(small_out)]
    for at, (_, n, p) in enumerate(order):
        stages[n](p)
        if n < 3 and p == pieces // 2:
            smalls[n]()


def write_kernel(first, second, small, first_out, second_out, bias_out, loss_out, first_buf, second_buf, sem):
    parts = first_buf.shape[0]
    rows = first_buf.shape[1]
    copies = [pltpu.make_async_copy(second_buf, second_out, sem.at[parts])]
    second_buf[...] = second[...].astype(jnp.float32)
    copies[0].start()
    for n in range(parts):
        at = pl.ds(n * rows, rows)
        first_buf[n] = first[at, :].astype(jnp.float32)
        copies.append(pltpu.make_async_copy(first_buf.at[n], first_out.at[at], sem.at[n]))
        copies[-1].start()
    hid = bias_out.shape[1]
    bias_out[...] = small[:, pl.ds(0, hid)]
    loss_out[...] = small[:, pl.ds(hid, 1)]
    for copy in copies:
        copy.wait()


def dot(lhs, rhs, dims):
    return lax.dot_general(lhs, rhs, (dims, ((), ())), preferred_element_type=jnp.float32)


def ideal_gain(counts, list_len):
    places = (1 + lax.broadcasted_iota(jnp.int32, (1, list_len), 1)).astype(jnp.float32)
    discount = log_two / jnp.log(1.0 + places)
    total = jnp.zeros((1, 1), jnp.float32)
    start = jnp.zeros((1, 1), jnp.float32)
    for level in reversed(range(len(gain_values))):
        finish = start + counts[level : level + 1, 0:1]
        inside = (places > start) & (places <= finish)
        total = total + gain_values[level] * jnp.sum(jnp.where(inside, discount, 0.0), axis=1, keepdims=True)
        start = finish
    return jnp.maximum(total, 1.0)


def step_kernel(
    chips, spans, lengths, labels_hbm, features_hbm, w_first_hbm, b_first_hbm, w_second_hbm,
    first_out, second_out, small_out,
    labels, b_first, feats, w_first, w_second, feats_t, hidden_t, pre, pre_other, hidden, keys, embs, slopes, ranks,
    label_rows, grad_emb, grad_pre,
    load_sem, key_s, key_r, label_s, label_r, mate_s, mate_r, *scratch,
):
    dp, span = lax.axis_index("dp"), lax.axis_index("span")
    core, chip = lax.rem(dp, 2), dp // 2
    place = (core, chip, span)
    rows, depth = feats.shape[1:]
    width = w_second.shape[1]
    hid = w_first.shape[1]
    half = hid // 2
    half_width = width // 2
    pair_scale = 1.0 / math.sqrt(half_width)
    list_count, list_len = 2 * chips, rows * spans
    loads = [
        pltpu.make_async_copy(src, dst, load_sem.at[n])
        for n, (src, dst) in enumerate(
            (
                (features_hbm.at[0], feats.at[0]), (w_first_hbm, w_first), (w_second_hbm, w_second),
                (labels_hbm, labels), (b_first_hbm, b_first),
            )
        )
    ]
    for load in loads:
        load.start()
    enter = greet_peers(place, chips, spans)

    def to_spans(refs, send, recv):
        made = []
        for k in range(1, spans):
            copy = pltpu.make_async_remote_copy(
                src_ref=refs.at[0], dst_ref=refs.at[k], send_sem=send.at[k - 1], recv_sem=recv.at[k - 1],
                device_id={"dp": dp, "span": lax.rem(span + k, spans)}, device_id_type=pl.DeviceIdType.MESH,
            )
            copy.start()
            made.append(copy)
        return made

    def to_mate(n, src, dst):
        copy = pltpu.make_async_remote_copy(
            src_ref=src, dst_ref=dst, send_sem=mate_s.at[n], recv_sem=mate_r.at[n],
            device_id={"dp": dp + 1 - 2 * core, "span": span}, device_id_type=pl.DeviceIdType.MESH,
        )
        copy.start()
        return copy

    length = lengths[0]
    my_half = pl.ds(pl.multiple_of(core * half, half), half)

    def live_at(k, shape, dim):
        owner = lax.rem(span - k + spans, spans)
        return (owner * rows + lax.broadcasted_iota(jnp.int32, shape, dim) < length).astype(jnp.float32)

    def live_row(k):
        return live_at(k, (1, rows), 1)

    def live_col(k):
        return live_at(k, (rows, 1), 0)

    loads[3].wait()
    label_rows[0] = labels[...].astype(jnp.float32)
    loads[4].wait()
    loads[0].wait()
    loads[1].wait()
    for p in range(hid // width):
        cols = pl.ds(p * width, width)
        pre_act = dot(feats[0], w_first[:, cols], ((1,), (0,))) + b_first[:, cols]
        pre[:, cols] = pre_act
        hidden[:, cols] = jnp.maximum(pre_act, 0.0).astype(jnp.bfloat16)
    loads[2].wait()
    row_emb = dot(hidden[...], w_second[...], ((1,), (0,))).astype(jnp.bfloat16)
    keys[0] = jnp.concatenate([row_emb[:, half_width:], -row_emb[:, :half_width]], axis=1)
    enter()
    label_copies = to_spans(label_rows, label_s, label_r)
    key_copies = to_spans(keys, key_s, key_r)
    feat_copy = to_mate(0, feats.at[0], feats.at[1])

    ranks[...] = jnp.zeros_like(ranks)

    def block(a, b, keep=False):
        above = jax.nn.sigmoid(dot(embs[a], keys[b], ((1,), (1,))) * pair_scale)
        ranks[b] += jnp.sum((above * live_col(a)).reshape(rows // 8, 8, rows), axis=0)
        if keep:
            slopes[b] = above * (1.0 - above)

    def meet(k):
        key_rows = keys[k]
        embs[k] = jnp.concatenate([-key_rows[:, half_width:], key_rows[:, :half_width]], axis=1)
        block(0, k, keep=True)
        if k:
            block(k, 0)
            block(k, k)

        def both(m, carry):
            block(m, k)
            block(k, m)
            return carry

        if k > 4:
            lax.fori_loop(1, k, both, 0)
        else:
            for m in range(1, k):
                both(m, 0)

    meet(0)
    feats_t[:, pl.ds(0, rows)] = feats[0].T
    hidden_t[:, pl.ds(0, rows)] = hidden[:, my_half].T
    feat_copy.wait()
    feats_t[:, pl.ds(rows, rows)] = feats[1].T
    other_act = dot(feats[1], w_first[:, my_half], ((1,), (0,))) + b_first[:, my_half]
    pre_other[...] = other_act
    hidden_t[:, pl.ds(rows, rows)] = jnp.maximum(other_act, 0.0).astype(jnp.bfloat16).T
    for copy in label_copies:
        copy.wait()
    levels = lax.broadcasted_iota(jnp.int32, (8, rows), 0).astype(jnp.float32)
    level_counts = jnp.zeros((8, 1), jnp.float32)
    for k in range(spans):
        level_counts = level_counts + jnp.sum(jnp.where(levels == label_rows[k], live_row(k), 0.0), axis=1, keepdims=True)
    ideal = ideal_gain(level_counts, list_len)
    for k in range(1, spans):
        key_copies[k - 1].wait()
        meet(k)

    def rank_weight(k):
        gain = jnp.zeros((1, rows), jnp.float32)
        for level, value in enumerate(gain_values):
            gain = gain + jnp.where(label_rows[k] == level, value, 0.0)
        gain = gain * live_row(k)
        rank = 0.5 + jnp.sum(ranks[k], axis=0, keepdims=True)
        log_rank = jnp.log(1.0 + rank)
        weight = gain / (ideal * list_count) * log_two / ((1.0 + rank) * log_rank * log_rank)
        return weight, gain * log_two / log_rank

    eye = lax.broadcasted_iota(jnp.int32, (rows, rows), 0) == lax.broadcasted_iota(jnp.int32, (rows, rows), 1)
    own_weight, own_dcg = rank_weight(0)
    weight_col = jnp.sum(jnp.where(eye, own_weight, 0.0), axis=1, keepdims=True)
    own_live = live_col(0)
    total = jnp.zeros((rows, width), jnp.float32)
    for k in range(spans):
        weight = rank_weight(k)[0] if k else own_weight
        pair_grad = slopes[k] * (own_live * weight - weight_col * live_row(k))
        total = total + dot(pair_grad.astype(jnp.bfloat16), keys[k], ((1,), (0,)))
    grad_emb[0] = (total * pair_scale).astype(jnp.bfloat16)
    emb_copy = to_mate(1, grad_emb.at[0], grad_emb.at[1])
    dcg = jnp.sum(own_dcg, axis=1, keepdims=True)
    loss_part = (1.0 / spans - dcg / ideal) / list_count

    def through(n, act):
        back = dot(grad_emb[n], w_second[my_half, :], ((1,), (1,)))
        grad_rows = jnp.where(act > 0.0, back, 0.0).astype(jnp.bfloat16)
        grad_pre[pl.ds(n * rows, rows), :] = grad_rows
        return jnp.sum(grad_rows.astype(jnp.float32), axis=0, keepdims=True)

    bias = through(0, pre[:, my_half])
    emb_copy.wait()

    span_rows = scratch[1].shape[1]
    second_pieces = half // span_rows
    first_chunks = depth // span_rows
    pieces = second_pieces + first_chunks * (half // width)

    def compute(p):
        if p < second_pieces:
            return dot(hidden_t[pl.ds(p * span_rows, span_rows), :], grad_emb[...].reshape(2 * rows, width), ((1,), (0,)))
        group, chunk = divmod(p - second_pieces, first_chunks)
        return dot(feats_t[pl.ds(chunk * span_rows, span_rows), :], grad_pre[:, pl.ds(group * width, width)], ((1,), (0,)))

    def result(p, side, start, size):
        if p < second_pieces:
            return second_out.at[rows_at(side * half + p * span_rows + start, size)]
        group, chunk = divmod(p - second_pieces, first_chunks)
        cols = pl.ds(pl.multiple_of(side * half + group * width, width), width)
        return first_out.at[rows_at(chunk * span_rows + start, size), cols]

    red = Reducer(place, chips, spans, pieces, compute, result, scratch)
    for p in range(second_pieces):
        red.chip_out(p)
    bias = bias + through(1, pre_other[...])
    red.small_first(jnp.concatenate([bias, jnp.broadcast_to(loss_part, (1, 128))], axis=1))
    for p in range(second_pieces, pieces):
        red.chip_out(p)
    finish_reduce(red, pieces, small_out)


def shards(features, lengths, labels, w_first, b_first, w_second):
    chips, spans = lax.axis_size("dp") // 2, lax.axis_size("span")
    rows, depth = features.shape[1:]
    hid, width = w_second.shape
    half = hid // 2
    piece_rows = min(512, half)
    pieces = (half + depth * (half // width)) // piece_rows
    small_width = half + 128
    vmem, dma = pltpu.VMEM, pltpu.SemaphoreType.DMA
    in_vmem = pl.BlockSpec(memory_space=pltpu.VMEM)
    in_place = pl.BlockSpec(memory_space=pl.ANY)
    in_hbm = pl.BlockSpec(memory_space=pltpu.HBM)
    first_sum, second_sum, small_sum = pl.pallas_call(
        lambda *refs: step_kernel(chips, spans, *refs),
        name="rank_step",
        out_shape=(
            jax.ShapeDtypeStruct((depth, hid), jnp.bfloat16),
            jax.ShapeDtypeStruct((hid, width), jnp.bfloat16),
            jax.ShapeDtypeStruct((1, hid + 128), jnp.float32),
        ),
        in_specs=[pl.BlockSpec(memory_space=pltpu.SMEM)] + [in_hbm] * 5,
        out_specs=(in_vmem,) * 3,
        scratch_shapes=[
            vmem((1, rows), jnp.int32),
            vmem((1, hid), jnp.float32),
            vmem((2, rows, depth), jnp.bfloat16),
            vmem((depth, hid), jnp.bfloat16),
            vmem((hid, width), jnp.bfloat16),
            vmem((depth, 2 * rows), jnp.bfloat16),
            vmem((half, 2 * rows), jnp.bfloat16),
            vmem((rows, hid), jnp.float32),
            vmem((rows, half), jnp.float32),
            vmem((rows, hid), jnp.bfloat16),
            vmem((spans, rows, width), jnp.bfloat16),
            vmem((spans, rows, width), jnp.bfloat16),
            vmem((spans, rows, rows), jnp.float32),
            vmem((spans, 8, rows), jnp.float32),
            vmem((spans, 1, rows), jnp.float32),
            vmem((2, rows, width), jnp.bfloat16),
            vmem((2 * rows, half), jnp.bfloat16),
            dma((5,)),
            dma((spans - 1,)), dma((spans - 1,)), dma((spans - 1,)), dma((spans - 1,)),
            dma((2,)), dma((2,)),
        ]
        + reducer_scratch(pieces, piece_rows, width, chips, spans, small_width),
        compiler_params=pltpu.CompilerParams(collective_id=0, has_side_effects=True, vmem_limit_bytes=40 << 20),
    )(lengths, *(pltpu.with_memory_space_constraint(x, pltpu.HBM) for x in (labels, features, w_first, b_first.reshape(1, -1), w_second)))
    parts = 4
    first, second, bias, loss = pl.pallas_call(
        write_kernel,
        name="write_out",
        out_shape=(
            jax.ShapeDtypeStruct((depth, hid), jnp.float32),
            jax.ShapeDtypeStruct((hid, width), jnp.float32),
            jax.ShapeDtypeStruct((1, hid), jnp.float32),
            jax.ShapeDtypeStruct((1, 1), jnp.float32),
        ),
        in_specs=[in_vmem] * 3,
        out_specs=(in_place, in_place, in_vmem, in_vmem),
        scratch_shapes=[
            vmem((parts, depth // parts, hid), jnp.float32),
            vmem((hid, width), jnp.float32),
            dma((parts + 1,)),
        ],
        compiler_params=pltpu.CompilerParams(vmem_limit_bytes=16 << 20),
    )(first_sum, second_sum, small_sum)
    return loss[0, 0], first, bias[0], second


def solution(mesh):
    placed = (P("dp", "span", None), P("dp"), P("dp", "span"), P(), P(), P())
    return jax.shard_map(
        shards, mesh=mesh, in_specs=placed, out_specs=(P(), P(), P(), P()), check_vma=False
    )
```

```python
import math

import jax
import jax.numpy as jnp
from jax import lax
from jax.experimental import pallas as pl
from jax.experimental.pallas import tpu as pltpu
from jax.sharding import PartitionSpec as P

gain_values = (0.0, 1.0, 3.0, 7.0, 15.0)
log_two = math.log(2.0)
piece_kinds = ("near", "far", "near", "near", "near")
piece_order = (
    0, 1, 2, 3, 4, 0, 2, 0, 1, 3, 2, 4, 1, 0, 3, 2, 4, 1, 3, 0,
    4, 3, 2, 1, 4, 3, 0, 2, 1, 4,
)


def greet_peers(place, chips, spans):
    core, chip, span = place
    barrier = pltpu.get_barrier_semaphore()
    peers = [{"dp": 2 * chip + 1 - core, "span": span}]
    peers += [{"dp": 2 * other_of(chip, k, chips) + core, "span": span} for k in range(1, chips)]
    peers += [{"dp": 2 * chip + core, "span": other_of(span, k, spans)} for k in range(1, spans)]
    for peer in peers:
        pl.semaphore_signal(barrier, inc=1, device_id=peer, device_id_type=pl.DeviceIdType.MESH)
    return lambda: pl.semaphore_wait(barrier, len(peers))


def other_of(me, k, count):
    if count & (count - 1):
        return lax.rem(me + k, count)
    bits = [1 << n for n in range(count.bit_length() - 1)]
    return me + sum((1 - 2 * lax.rem(me // bit, 2)) * (k // bit % 2 * bit) for bit in bits)


def owner_of(me, k, count):
    if count & (count - 1):
        return lax.rem(me - k + count, count)
    return other_of(me, k, count)


def rows_at(start, size):
    return pl.ds(pl.multiple_of(start, size), size)


def owners_of(rows, chips, spans):
    return min(spans, rows // chips // 16)


class Reducer:
    def __init__(self, place, chips, spans, plan, compute, result, scratch):
        self.core, self.chip, self.span = place
        self.chips, self.spans = chips, spans
        self.compute, self.result = compute, result
        (
            self.full_sum, self.buf, self.chip_in, self.span_in,
            self.small_chip, self.small_span, self.small_pair,
            self.pair_s, self.pair_r, self.chip_s, self.chip_r, self.span_s, self.span_r,
            self.small_s, self.small_r,
        ) = scratch
        self.rows = self.buf.shape[1]
        self.block = self.rows // chips
        self.owners = owners_of(self.rows, chips, spans)
        self.part = self.block // self.owners
        self.copies = {}
        self.chip_steps = sorted(range(1, chips), key=lambda k: (-bin(k).count("1"), k))
        far = self.rows // spans // chips >= 16
        near = (self.near_out, self.near_span, self.near_back, self.near_chip, self.pair_back, self.last)
        every = (self.near_out, self.every_span, self.every_chip, self.pair_back, self.last)
        remote = (self.far_out, self.far_chip, self.far_back, self.far_span, self.pair_back, self.last)
        self.stages = [{"near": near, "every": every, "far": remote if far else near}[kind] for kind in plan]
        self.at = [0] * len(plan)

    def advance(self, p):
        self.stages[p][self.at[p]](p)
        self.at[p] += 1

    def copy(self, key, src, dst, send, recv, dp=None, span=None):
        peer = {
            "dp": 2 * self.chip + self.core if dp is None else dp,
            "span": self.span if span is None else span,
        }
        made = pltpu.make_async_remote_copy(
            src_ref=src, dst_ref=dst, send_sem=send, recv_sem=recv,
            device_id=peer, device_id_type=pl.DeviceIdType.MESH,
        )
        made.start()
        self.copies.setdefault(key, []).append(made)

    def to_chip(self, p, n, k, src, dst):
        self.copy(p, src, dst, self.chip_s.at[n, p, k - 1], self.chip_r.at[n, p, k - 1], dp=self.other_chip(k))

    def to_span(self, p, n, k, src, dst):
        self.copy(p, src, dst, self.span_s.at[n, p, k - 1], self.span_r.at[n, p, k - 1], span=self.other_span(k))

    def settle(self, key):
        for made in self.copies.pop(key, []):
            made.wait()

    def partner(self):
        return 2 * self.chip + 1 - self.core

    def other_chip(self, k):
        return 2 * other_of(self.chip, k, self.chips) + self.core

    def other_span(self, k):
        return other_of(self.span, k, self.spans)

    def begin(self, p):
        total = self.compute(p)
        self.full_sum[p] = total
        self.buf[p] = total.astype(jnp.bfloat16)

    def gathered(self, p, mine, arrived, count, size):
        self.settle(p)
        total = self.full_sum[p, mine]
        for k in range(count):
            total = total + arrived[p, pl.ds(k * size, size)].astype(jnp.float32)
        return total

    def spread_chips(self, p, base):
        for k in self.chip_steps:
            rows = rows_at(base + other_of(self.chip, k, self.chips) * self.block, self.block)
            self.to_chip(p, 0, k, self.buf.at[p, rows], self.chip_in.at[p, pl.ds((k - 1) * self.block, self.block)])

    def near_out(self, p):
        self.begin(p)
        self.spread_chips(p, 0)

    def near_sum(self, p):
        return self.gathered(p, rows_at(self.chip * self.block, self.block), self.chip_in, self.chips - 1, self.block)

    def near_span(self, p):
        total = self.near_sum(p)
        mine = rows_at(self.chip * self.block, self.block)
        self.full_sum[p, mine] = total
        self.buf[p, mine] = total.astype(jnp.bfloat16)
        for k in range(1, self.spans):
            to = self.other_span(k)
            rows = rows_at(self.chip * self.block + lax.rem(to, self.owners) * self.part, self.part)
            self.to_span(p, 0, k, self.buf.at[p, rows], self.span_in.at[p, pl.ds((k - 1) * self.part, self.part)])

    def near_back(self, p):
        mine = lax.rem(self.span, self.owners)
        start = self.chip * self.block + mine * self.part
        rows = rows_at(start, self.part)
        if self.owners < self.spans:
            self.full_sum[p, rows] = self.buf[p, rows].astype(jnp.float32)
        total = self.gathered(p, rows, self.span_in, self.spans - 1, self.part)
        place = self.result(p, self.core, start, self.part)
        place[...] = total.astype(jnp.bfloat16)
        for k in range(1, self.owners):
            to = self.span - mine + other_of(mine, k, self.owners)
            self.copy(p, place, place, self.span_s.at[1, p, k - 1], self.span_r.at[1, p, k - 1], span=to)

    def back_chips(self, p, start):
        place = self.result(p, self.core, start, self.block)
        for k in self.chip_steps:
            self.to_chip(p, 1, k, place, place)

    def near_chip(self, p):
        self.settle(p)
        self.back_chips(p, self.chip * self.block)

    def every_span(self, p):
        slot = self.span_in.at[p, rows_at(self.span * self.block, self.block)]
        slot[...] = self.near_sum(p).astype(jnp.bfloat16)
        for k in range(1, self.spans):
            self.to_span(p, 0, k, slot, slot)

    def every_chip(self, p):
        self.settle(p)
        total = self.span_in[p, pl.ds(0, self.block)].astype(jnp.float32)
        for k in range(1, self.spans):
            total = total + self.span_in[p, pl.ds(k * self.block, self.block)].astype(jnp.float32)
        self.result(p, self.core, self.chip * self.block, self.block)[...] = total.astype(jnp.bfloat16)
        self.back_chips(p, self.chip * self.block)

    def far_out(self, p):
        self.begin(p)
        size = self.rows // self.spans
        for k in range(1, self.spans):
            rows = rows_at(self.other_span(k) * size, size)
            self.to_span(p, 0, k, self.buf.at[p, rows], self.span_in.at[p, pl.ds((k - 1) * size, size)])

    def far_chip(self, p):
        size = self.rows // self.spans
        mine = rows_at(self.span * size, size)
        total = self.gathered(p, mine, self.span_in, self.spans - 1, size)
        self.full_sum[p, mine] = total
        self.buf[p, mine] = total.astype(jnp.bfloat16)
        small = size // self.chips
        for k in self.chip_steps:
            rows = rows_at(self.span * size + other_of(self.chip, k, self.chips) * small, small)
            self.to_chip(p, 0, k, self.buf.at[p, rows], self.chip_in.at[p, pl.ds((k - 1) * small, small)])

    def far_back(self, p):
        size = self.rows // self.spans
        small = size // self.chips
        start = self.span * size + self.chip * small
        total = self.gathered(p, rows_at(start, small), self.chip_in, self.chips - 1, small)
        place = self.result(p, self.core, start, small)
        place[...] = total.astype(jnp.bfloat16)
        for k in self.chip_steps:
            self.to_chip(p, 1, k, place, place)

    def far_span(self, p):
        self.settle(p)
        size = self.rows // self.spans
        place = self.result(p, self.core, self.span * size, size)
        for k in range(1, self.spans):
            self.to_span(p, 1, k, place, place)

    def pair_back(self, p):
        self.settle(p)
        place = self.result(p, self.core, 0, self.rows)
        self.copy(p, place, place, self.pair_s.at[p], self.pair_r.at[p], dp=self.partner())

    def last(self, p):
        self.settle(p)

    def small_first(self, values):
        self.small_chip[self.chip] = values
        place = self.small_chip.at[self.chip]
        for k in range(1, self.chips):
            self.copy("small0", place, place, self.small_s.at[k - 1], self.small_r.at[k - 1], dp=self.other_chip(k))

    def small_second(self):
        self.settle("small0")
        total = self.small_chip[0]
        for k in range(1, self.chips):
            total = total + self.small_chip[k]
        self.small_span[self.span] = total
        place = self.small_span.at[self.span]
        for k in range(1, self.spans):
            at = self.chips + k - 2
            self.copy("small1", place, place, self.small_s.at[at], self.small_r.at[at], span=self.other_span(k))

    def small_third(self):
        self.settle("small1")
        total = self.small_span[0]
        for k in range(1, self.spans):
            total = total + self.small_span[k]
        self.small_pair[self.core] = total
        place = self.small_pair.at[self.core]
        at = self.chips + self.spans - 2
        self.copy("small2", place, place, self.small_s.at[at], self.small_r.at[at], dp=self.partner())

    def small_last(self, out):
        self.settle("small2")
        half = self.small_pair.shape[2] - 128
        for c in range(2):
            out[:, pl.ds(c * half, half)] = self.small_pair[c, :, pl.ds(0, half)]
        out[:, pl.ds(2 * half, 128)] = self.small_pair[0, :, pl.ds(half, 128)] + self.small_pair[1, :, pl.ds(half, 128)]


def reducer_scratch(pieces, rows, width, chips, spans, small_width):
    vmem, dma = pltpu.VMEM, pltpu.SemaphoreType.DMA
    return [
        vmem((pieces, rows, width), jnp.float32),
        vmem((pieces, rows, width), jnp.bfloat16),
        vmem((pieces, rows, width), jnp.bfloat16),
        vmem((pieces, max(rows, spans * rows // chips), width), jnp.bfloat16),
        vmem((chips, 1, small_width), jnp.float32),
        vmem((spans, 1, small_width), jnp.float32),
        vmem((2, 1, small_width), jnp.float32),
        dma((pieces,)), dma((pieces,)),
        dma((2, pieces, chips - 1)), dma((2, pieces, chips - 1)),
        dma((2, pieces, spans - 1)), dma((2, pieces, spans - 1)),
        dma((chips + spans - 1,)), dma((chips + spans - 1,)),
    ]


def write_kernel(first, second, small, first_out, second_out, bias_out, loss_out, first_buf, second_buf, sem):
    parts = first_buf.shape[0]
    rows = first_buf.shape[1]
    copies = [pltpu.make_async_copy(second_buf, second_out, sem.at[parts])]
    second_buf[...] = second[...].astype(jnp.float32)
    copies[0].start()
    for n in range(parts):
        at = pl.ds(n * rows, rows)
        first_buf[n] = first[at, :].astype(jnp.float32)
        copies.append(pltpu.make_async_copy(first_buf.at[n], first_out.at[at], sem.at[n]))
        copies[-1].start()
    hid = bias_out.shape[1]
    bias_out[...] = small[:, pl.ds(0, hid)]
    loss_out[...] = small[:, pl.ds(hid, 1)]
    for copy in copies:
        copy.wait()


def dot(lhs, rhs, dims):
    return lax.dot_general(lhs, rhs, (dims, ((), ())), preferred_element_type=jnp.float32)


def ideal_gain(counts, list_len):
    places = (1 + lax.broadcasted_iota(jnp.int32, (1, list_len), 1)).astype(jnp.float32)
    discount = log_two / jnp.log(1.0 + places)
    total = jnp.zeros((1, 1), jnp.float32)
    start = jnp.zeros((1, 1), jnp.float32)
    for level in reversed(range(len(gain_values))):
        finish = start + counts[level : level + 1, 0:1]
        inside = (places > start) & (places <= finish)
        total = total + gain_values[level] * jnp.sum(jnp.where(inside, discount, 0.0), axis=1, keepdims=True)
        start = finish
    return jnp.maximum(total, 1.0)


def relay_keys(span, keys, send, recv):
    parts = 4
    size = keys.shape[1] // parts

    def made(n, src, dst, k):
        return pltpu.make_async_remote_copy(
            src_ref=src, dst_ref=dst, send_sem=send.at[n], recv_sem=recv.at[n],
            device_id={"dp": lax.axis_index("dp"), "span": other_of(span, k, 4)}, device_id_type=pl.DeviceIdType.MESH,
        )

    blocks = [pl.ds(n * size, size) for n in range(parts)]
    far = [made(n, keys.at[0, at], keys.at[2, at], 2) for n, at in enumerate(blocks)]
    passed = [made(parts + n, keys.at[2, at], keys.at[3, at], 1) for n, at in enumerate(blocks)]
    mid = made(2 * parts, keys.at[0], keys.at[3], 3)
    near = made(2 * parts + 1, keys.at[0], keys.at[1], 1)
    return far, mid, near, passed


def step_kernel(
    chips, spans, lengths, labels_hbm, features_hbm, w_first_hbm, b_first_hbm, w_second_hbm,
    first_out, second_out, small_out,
    labels, b_first, feats, w_first, w_second, feats_t, hidden_t, pre, pre_other, hidden, keys, embs, slopes, ranks,
    label_rows, grad_emb, grad_pre,
    load_sem, key_s, key_r, label_s, label_r, mate_s, mate_r, *scratch,
):
    dp, span = lax.axis_index("dp"), lax.axis_index("span")
    core, chip = lax.rem(dp, 2), dp // 2
    place = (core, chip, span)
    rows, depth = feats.shape[1:]
    width = w_second.shape[1]
    hid = w_first.shape[1]
    half = hid // 2
    half_width = width // 2
    pair_scale = 1.0 / math.sqrt(half_width)
    list_count, list_len = 2 * chips, rows * spans
    loads = [
        pltpu.make_async_copy(src, dst, load_sem.at[n])
        for n, (src, dst) in enumerate(
            (
                (features_hbm.at[0], feats.at[0]), (w_first_hbm, w_first), (w_second_hbm, w_second),
                (labels_hbm, labels), (b_first_hbm, b_first),
            )
        )
    ]
    for load in loads:
        load.start()
    enter = greet_peers(place, chips, spans)

    def to_spans(refs, send, recv):
        made = []
        for k in range(1, spans):
            copy = pltpu.make_async_remote_copy(
                src_ref=refs.at[0], dst_ref=refs.at[k], send_sem=send.at[k - 1], recv_sem=recv.at[k - 1],
                device_id={"dp": dp, "span": other_of(span, k, spans)}, device_id_type=pl.DeviceIdType.MESH,
            )
            copy.start()
            made.append(copy)
        return made

    def to_mate(n, src, dst):
        copy = pltpu.make_async_remote_copy(
            src_ref=src, dst_ref=dst, send_sem=mate_s.at[n], recv_sem=mate_r.at[n],
            device_id={"dp": dp + 1 - 2 * core, "span": span}, device_id_type=pl.DeviceIdType.MESH,
        )
        copy.start()
        return copy

    length = lengths[0]
    my_half = pl.ds(pl.multiple_of(core * half, half), half)

    def live_at(k, shape, dim):
        owner = owner_of(span, k, spans)
        return (owner * rows + lax.broadcasted_iota(jnp.int32, shape, dim) < length).astype(jnp.float32)

    def live_row(k):
        return live_at(k, (1, rows), 1)

    def live_col(k):
        return live_at(k, (rows, 1), 0)

    loads[3].wait()
    label_rows[0] = labels[...].astype(jnp.float32)
    loads[4].wait()
    loads[0].wait()
    loads[1].wait()
    for p in range(hid // width):
        cols = pl.ds(p * width, width)
        pre_act = dot(feats[0], w_first[:, cols], ((1,), (0,))) + b_first[:, cols]
        pre[:, cols] = pre_act
        hidden[:, cols] = jnp.maximum(pre_act, 0.0).astype(jnp.bfloat16)
    loads[2].wait()
    row_emb = dot(hidden[...], w_second[...], ((1,), (0,))).astype(jnp.bfloat16)
    keys[0] = jnp.concatenate([row_emb[:, half_width:], -row_emb[:, :half_width]], axis=1)
    enter()
    label_copies = to_spans(label_rows, label_s, label_r)
    if spans == 4:
        far_keys, mid_key, near_key, passed = relay_keys(span, keys, key_s, key_r)
        inner = lax.rem((span + 1) // 2, 2) == 1
        for copy in far_keys:
            copy.start()
        near_key.start()
        pl.when(inner)(mid_key.start)
    else:
        key_copies = to_spans(keys, key_s, key_r)
    feat_copy = to_mate(0, feats.at[0], feats.at[1])

    ranks[...] = jnp.zeros_like(ranks)

    def block(a, b, keep=False):
        above = jax.nn.sigmoid(dot(embs[a], keys[b], ((1,), (1,))) * pair_scale)
        ranks[b] += jnp.sum((above * live_col(a)).reshape(rows // 8, 8, rows), axis=0)
        if keep:
            slopes[b] = above * (1.0 - above)

    def meet(k):
        key_rows = keys[k]
        embs[k] = jnp.concatenate([-key_rows[:, half_width:], key_rows[:, :half_width]], axis=1)
        block(0, k, keep=True)
        if k:
            block(k, 0)
            block(k, k)

        def both(m, carry):
            block(m, k)
            block(k, m)
            return carry

        if k > 4:
            lax.fori_loop(1, k, both, 0)
        else:
            for m in range(1, k):
                both(m, 0)

    meet(0)
    feats_t[:, pl.ds(0, rows)] = feats[0].T
    hidden_t[:, pl.ds(0, rows)] = hidden[:, my_half].T
    feat_copy.wait()
    feats_t[:, pl.ds(rows, rows)] = feats[1].T
    other_act = dot(feats[1], w_first[:, my_half], ((1,), (0,))) + b_first[:, my_half]
    pre_other[...] = other_act
    hidden_t[:, pl.ds(rows, rows)] = jnp.maximum(other_act, 0.0).astype(jnp.bfloat16).T
    for copy in label_copies:
        copy.wait()
    levels = lax.broadcasted_iota(jnp.int32, (8, rows), 0).astype(jnp.float32)
    level_counts = jnp.zeros((8, 1), jnp.float32)
    for k in range(spans):
        level_counts = level_counts + jnp.sum(jnp.where(levels == label_rows[k], live_row(k), 0.0), axis=1, keepdims=True)
    ideal = ideal_gain(level_counts, list_len)
    if spans == 4:
        for copy, onward in zip(far_keys, passed):
            copy.wait_recv()
            pl.when(inner)(onward.start)
        near_key.wait_recv()
        meet(1)
        meet(2)
        pl.when(inner)(mid_key.wait)

        @pl.when(jnp.logical_not(inner))
        def _():
            for onward in passed:
                onward.wait_recv()

        meet(3)
    else:
        for k in range(1, spans):
            key_copies[k - 1].wait()
            meet(k)

    def rank_weight(k):
        gain = jnp.zeros((1, rows), jnp.float32)
        for level, value in enumerate(gain_values):
            gain = gain + jnp.where(label_rows[k] == level, value, 0.0)
        gain = gain * live_row(k)
        rank = 0.5 + jnp.sum(ranks[k], axis=0, keepdims=True)
        log_rank = jnp.log(1.0 + rank)
        weight = gain / (ideal * list_count) * log_two / ((1.0 + rank) * log_rank * log_rank)
        return weight, gain * log_two / log_rank

    eye = lax.broadcasted_iota(jnp.int32, (rows, rows), 0) == lax.broadcasted_iota(jnp.int32, (rows, rows), 1)
    own_weight, own_dcg = rank_weight(0)
    weight_col = jnp.sum(jnp.where(eye, own_weight, 0.0), axis=1, keepdims=True)
    own_live = live_col(0)
    total = jnp.zeros((rows, width), jnp.float32)
    for k in range(spans):
        weight = rank_weight(k)[0] if k else own_weight
        pair_grad = slopes[k] * (own_live * weight - weight_col * live_row(k))
        total = total + dot(pair_grad.astype(jnp.bfloat16), keys[k], ((1,), (0,)))
    grad_emb[0] = (total * pair_scale).astype(jnp.bfloat16)
    emb_copy = to_mate(1, grad_emb.at[0], grad_emb.at[1])
    if spans == 4:
        for copy in far_keys + [near_key]:
            copy.wait_send()

        @pl.when(inner)
        def _():
            for onward in passed:
                onward.wait_send()

    dcg = jnp.sum(own_dcg, axis=1, keepdims=True)
    loss_part = (1.0 / spans - dcg / ideal) / list_count

    def through(n, act):
        back = dot(grad_emb[n], w_second[my_half, :], ((1,), (1,)))
        grad_rows = jnp.where(act > 0.0, back, 0.0).astype(jnp.bfloat16)
        grad_pre[pl.ds(n * rows, rows), :] = grad_rows
        return jnp.sum(grad_rows.astype(jnp.float32), axis=0, keepdims=True)

    bias = through(0, pre[:, my_half])
    emb_copy.wait()

    span_rows = scratch[1].shape[1]
    second_pieces = half // span_rows
    first_chunks = depth // span_rows
    pieces = second_pieces + first_chunks * (half // width)

    def compute(p):
        if p < second_pieces:
            return dot(hidden_t[pl.ds(p * span_rows, span_rows), :], grad_emb[...].reshape(2 * rows, width), ((1,), (0,)))
        group, chunk = divmod(p - second_pieces, first_chunks)
        return dot(feats_t[pl.ds(chunk * span_rows, span_rows), :], grad_pre[:, pl.ds(group * width, width)], ((1,), (0,)))

    def result(p, side, start, size):
        if p < second_pieces:
            return second_out.at[rows_at(side * half + p * span_rows + start, size)]
        group, chunk = divmod(p - second_pieces, first_chunks)
        cols = pl.ds(pl.multiple_of(side * half + group * width, width), width)
        return first_out.at[rows_at(chunk * span_rows + start, size), cols]

    if pieces != len(piece_kinds):
        kinds = ("near",) * pieces
        order = [p for n in range(6) for p in range(pieces)]
    else:
        kinds, order = piece_kinds, piece_order
    red = Reducer(place, chips, spans, kinds, compute, result, scratch)
    bias_after = second_pieces
    smalls = {3 * pieces: red.small_second, 4 * pieces: red.small_third}
    for n, p in enumerate(order):
        if red.at[p] == 0 and p == bias_after:
            bias = bias + through(1, pre_other[...])
            red.small_first(jnp.concatenate([bias, jnp.broadcast_to(loss_part, (1, 128))], axis=1))
        red.advance(p)
        if n in smalls:
            smalls[n]()
    red.small_last(small_out)


def shards(features, lengths, labels, w_first, b_first, w_second):
    chips, spans = lax.axis_size("dp") // 2, lax.axis_size("span")
    rows, depth = features.shape[1:]
    hid, width = w_second.shape
    half = hid // 2
    piece_rows = min(512, half)
    pieces = (half + depth * (half // width)) // piece_rows
    small_width = half + 128
    vmem, dma = pltpu.VMEM, pltpu.SemaphoreType.DMA
    in_vmem = pl.BlockSpec(memory_space=pltpu.VMEM)
    in_place = pl.BlockSpec(memory_space=pl.ANY)
    in_hbm = pl.BlockSpec(memory_space=pltpu.HBM)
    first_sum, second_sum, small_sum = pl.pallas_call(
        lambda *refs: step_kernel(chips, spans, *refs),
        name="rank_step",
        out_shape=(
            jax.ShapeDtypeStruct((depth, hid), jnp.bfloat16),
            jax.ShapeDtypeStruct((hid, width), jnp.bfloat16),
            jax.ShapeDtypeStruct((1, hid + 128), jnp.float32),
        ),
        in_specs=[pl.BlockSpec(memory_space=pltpu.SMEM)] + [in_hbm] * 5,
        out_specs=(in_vmem,) * 3,
        scratch_shapes=[
            vmem((1, rows), jnp.int32),
            vmem((1, hid), jnp.float32),
            vmem((2, rows, depth), jnp.bfloat16),
            vmem((depth, hid), jnp.bfloat16),
            vmem((hid, width), jnp.bfloat16),
            vmem((depth, 2 * rows), jnp.bfloat16),
            vmem((half, 2 * rows), jnp.bfloat16),
            vmem((rows, hid), jnp.float32),
            vmem((rows, half), jnp.float32),
            vmem((rows, hid), jnp.bfloat16),
            vmem((spans, rows, width), jnp.bfloat16),
            vmem((spans, rows, width), jnp.bfloat16),
            vmem((spans, rows, rows), jnp.float32),
            vmem((spans, 8, rows), jnp.float32),
            vmem((spans, 1, rows), jnp.float32),
            vmem((2, rows, width), jnp.bfloat16),
            vmem((2 * rows, half), jnp.bfloat16),
            dma((5,)),
            dma((spans + 9,)), dma((spans + 9,)), dma((spans - 1,)), dma((spans - 1,)),
            dma((2,)), dma((2,)),
        ]
        + reducer_scratch(pieces, piece_rows, width, chips, spans, small_width),
        compiler_params=pltpu.CompilerParams(collective_id=0, has_side_effects=True, vmem_limit_bytes=40 << 20),
    )(lengths, *(pltpu.with_memory_space_constraint(x, pltpu.HBM) for x in (labels, features, w_first, b_first.reshape(1, -1), w_second)))
    parts = 4
    first, second, bias, loss = pl.pallas_call(
        write_kernel,
        name="write_out",
        out_shape=(
            jax.ShapeDtypeStruct((depth, hid), jnp.float32),
            jax.ShapeDtypeStruct((hid, width), jnp.float32),
            jax.ShapeDtypeStruct((1, hid), jnp.float32),
            jax.ShapeDtypeStruct((1, 1), jnp.float32),
        ),
        in_specs=[in_vmem] * 3,
        out_specs=(in_place, in_place, in_vmem, in_vmem),
        scratch_shapes=[
            vmem((parts, depth // parts, hid), jnp.float32),
            vmem((hid, width), jnp.float32),
            dma((parts + 1,)),
        ],
        compiler_params=pltpu.CompilerParams(vmem_limit_bytes=16 << 20),
    )(first_sum, second_sum, small_sum)
    return loss[0, 0], first, bias[0], second


def solution(mesh):
    placed = (P("dp", "span", None), P("dp"), P("dp", "span"), P(), P(), P())
    return jax.shard_map(
        shards, mesh=mesh, in_specs=placed, out_specs=(P(), P(), P(), P()), check_vma=False
    )
```

```python
import math

import jax
import jax.numpy as jnp
from jax import lax
from jax.experimental import pallas as pl
from jax.experimental.pallas import tpu as pltpu
from jax.sharding import PartitionSpec as P

gain_values = (0.0, 1.0, 3.0, 7.0, 15.0)
log_two = math.log(2.0)
piece_plan = ((512, "near"), (512, "far"), (512, "near"), (512, "near"), (256, "near"), (256, "near"))
piece_order = (
    0, 1, 2, 3, 0, 2, 4, 1, 0, 5, 3, 2, 4, 1, 5, 0, 3, 2, 4, 5,
    1, 3, 0, 5, 4, 0, 3, 2, 1, 5, 3, 4, 1, 5, 2, 4,
)


def greet_peers(place, chips, spans):
    core, chip, span = place
    barrier = pltpu.get_barrier_semaphore()
    peers = [{"dp": 2 * chip + 1 - core, "span": span}]
    peers += [{"dp": 2 * other_of(chip, k, chips) + core, "span": span} for k in range(1, chips)]
    peers += [{"dp": 2 * chip + core, "span": other_of(span, k, spans)} for k in range(1, spans)]
    for peer in peers:
        pl.semaphore_signal(barrier, inc=1, device_id=peer, device_id_type=pl.DeviceIdType.MESH)
    return lambda: pl.semaphore_wait(barrier, len(peers))


def other_of(me, k, count):
    if count & (count - 1):
        return lax.rem(me + k, count)
    bits = [1 << n for n in range(count.bit_length() - 1)]
    return me + sum((1 - 2 * lax.rem(me // bit, 2)) * (k // bit % 2 * bit) for bit in bits)


def owner_of(me, k, count):
    if count & (count - 1):
        return lax.rem(me - k + count, count)
    return other_of(me, k, count)


def rows_at(start, size):
    return pl.ds(pl.multiple_of(start, size), size)


def owners_of(rows, chips, spans):
    return min(spans, rows // chips // 16)


class Reducer:
    def __init__(self, place, chips, spans, plan, compute, result, scratch):
        self.core, self.chip, self.span = place
        self.chips, self.spans = chips, spans
        self.compute, self.result = compute, result
        (
            self.full_sum, self.buf, self.chip_in, self.span_in,
            self.small_chip, self.small_span, self.small_pair,
            self.pair_s, self.pair_r, self.chip_s, self.chip_r, self.span_s, self.span_r,
            self.small_s, self.small_r,
        ) = scratch
        self.rows = [size for size, _ in plan]
        self.block = [size // chips for size in self.rows]
        self.owners = [owners_of(size, chips, spans) for size in self.rows]
        self.part = [block // owners for block, owners in zip(self.block, self.owners)]
        self.copies = {}
        self.chip_steps = sorted(range(1, chips), key=lambda k: (-bin(k).count("1"), k))
        far = [size // spans // chips >= 16 for size in self.rows]
        near = (self.near_out, self.near_span, self.near_back, self.near_chip, self.pair_back, self.last)
        every = (self.near_out, self.every_span, self.every_chip, self.pair_back, self.last)
        remote = (self.far_out, self.far_chip, self.far_back, self.far_span, self.pair_back, self.last)
        self.stages = [{"near": near, "every": every, "far": remote if far[p] else near}[kind] for p, (_, kind) in enumerate(plan)]
        self.at = [0] * len(plan)

    def advance(self, p):
        self.stages[p][self.at[p]](p)
        self.at[p] += 1

    def copy(self, key, src, dst, send, recv, dp=None, span=None):
        peer = {
            "dp": 2 * self.chip + self.core if dp is None else dp,
            "span": self.span if span is None else span,
        }
        made = pltpu.make_async_remote_copy(
            src_ref=src, dst_ref=dst, send_sem=send, recv_sem=recv,
            device_id=peer, device_id_type=pl.DeviceIdType.MESH,
        )
        made.start()
        self.copies.setdefault(key, []).append(made)

    def to_chip(self, p, n, k, src, dst):
        self.copy(p, src, dst, self.chip_s.at[n, p, k - 1], self.chip_r.at[n, p, k - 1], dp=self.other_chip(k))

    def to_span(self, p, n, k, src, dst):
        self.copy(p, src, dst, self.span_s.at[n, p, k - 1], self.span_r.at[n, p, k - 1], span=self.other_span(k))

    def settle(self, key):
        for made in self.copies.pop(key, []):
            made.wait()

    def partner(self):
        return 2 * self.chip + 1 - self.core

    def other_chip(self, k):
        return 2 * other_of(self.chip, k, self.chips) + self.core

    def other_span(self, k):
        return other_of(self.span, k, self.spans)

    def begin(self, p):
        total = self.compute(p)
        rows = pl.ds(0, self.rows[p])
        self.full_sum[p, rows] = total
        self.buf[p, rows] = total.astype(jnp.bfloat16)

    def gathered(self, p, mine, arrived, count, size):
        self.settle(p)
        total = self.full_sum[p, mine]
        for k in range(count):
            total = total + arrived[p, pl.ds(k * size, size)].astype(jnp.float32)
        return total

    def spread_chips(self, p, base):
        for k in self.chip_steps:
            rows = rows_at(base + other_of(self.chip, k, self.chips) * self.block[p], self.block[p])
            self.to_chip(p, 0, k, self.buf.at[p, rows], self.chip_in.at[p, pl.ds((k - 1) * self.block[p], self.block[p])])

    def near_out(self, p):
        self.begin(p)
        self.spread_chips(p, 0)

    def near_sum(self, p):
        return self.gathered(p, rows_at(self.chip * self.block[p], self.block[p]), self.chip_in, self.chips - 1, self.block[p])

    def near_span(self, p):
        total = self.near_sum(p)
        mine = rows_at(self.chip * self.block[p], self.block[p])
        self.full_sum[p, mine] = total
        self.buf[p, mine] = total.astype(jnp.bfloat16)
        for k in range(1, self.spans):
            to = self.other_span(k)
            rows = rows_at(self.chip * self.block[p] + lax.rem(to, self.owners[p]) * self.part[p], self.part[p])
            self.to_span(p, 0, k, self.buf.at[p, rows], self.span_in.at[p, pl.ds((k - 1) * self.part[p], self.part[p])])

    def near_back(self, p):
        mine = lax.rem(self.span, self.owners[p])
        start = self.chip * self.block[p] + mine * self.part[p]
        rows = rows_at(start, self.part[p])
        if self.owners[p] < self.spans:
            self.full_sum[p, rows] = self.buf[p, rows].astype(jnp.float32)
        total = self.gathered(p, rows, self.span_in, self.spans - 1, self.part[p])
        place = self.result(p, self.core, start, self.part[p])
        place[...] = total.astype(jnp.bfloat16)
        for k in range(1, self.owners[p]):
            to = self.span - mine + other_of(mine, k, self.owners[p])
            self.copy(p, place, place, self.span_s.at[1, p, k - 1], self.span_r.at[1, p, k - 1], span=to)

    def back_chips(self, p, start):
        place = self.result(p, self.core, start, self.block[p])
        for k in self.chip_steps:
            self.to_chip(p, 1, k, place, place)

    def near_chip(self, p):
        self.settle(p)
        self.back_chips(p, self.chip * self.block[p])

    def every_span(self, p):
        slot = self.span_in.at[p, rows_at(self.span * self.block[p], self.block[p])]
        slot[...] = self.near_sum(p).astype(jnp.bfloat16)
        for k in range(1, self.spans):
            self.to_span(p, 0, k, slot, slot)

    def every_chip(self, p):
        self.settle(p)
        total = self.span_in[p, pl.ds(0, self.block[p])].astype(jnp.float32)
        for k in range(1, self.spans):
            total = total + self.span_in[p, pl.ds(k * self.block[p], self.block[p])].astype(jnp.float32)
        self.result(p, self.core, self.chip * self.block[p], self.block[p])[...] = total.astype(jnp.bfloat16)
        self.back_chips(p, self.chip * self.block[p])

    def far_out(self, p):
        self.begin(p)
        size = self.rows[p] // self.spans
        for k in range(1, self.spans):
            rows = rows_at(self.other_span(k) * size, size)
            self.to_span(p, 0, k, self.buf.at[p, rows], self.span_in.at[p, pl.ds((k - 1) * size, size)])

    def far_chip(self, p):
        size = self.rows[p] // self.spans
        mine = rows_at(self.span * size, size)
        total = self.gathered(p, mine, self.span_in, self.spans - 1, size)
        self.full_sum[p, mine] = total
        self.buf[p, mine] = total.astype(jnp.bfloat16)
        small = size // self.chips
        for k in self.chip_steps:
            rows = rows_at(self.span * size + other_of(self.chip, k, self.chips) * small, small)
            self.to_chip(p, 0, k, self.buf.at[p, rows], self.chip_in.at[p, pl.ds((k - 1) * small, small)])

    def far_back(self, p):
        size = self.rows[p] // self.spans
        small = size // self.chips
        start = self.span * size + self.chip * small
        total = self.gathered(p, rows_at(start, small), self.chip_in, self.chips - 1, small)
        place = self.result(p, self.core, start, small)
        place[...] = total.astype(jnp.bfloat16)
        for k in self.chip_steps:
            self.to_chip(p, 1, k, place, place)

    def far_span(self, p):
        self.settle(p)
        size = self.rows[p] // self.spans
        place = self.result(p, self.core, self.span * size, size)
        for k in range(1, self.spans):
            self.to_span(p, 1, k, place, place)

    def pair_back(self, p):
        self.settle(p)
        place = self.result(p, self.core, 0, self.rows[p])
        self.copy(p, place, place, self.pair_s.at[p], self.pair_r.at[p], dp=self.partner())

    def last(self, p):
        self.settle(p)

    def small_first(self, values):
        self.small_chip[self.chip] = values
        place = self.small_chip.at[self.chip]
        for k in range(1, self.chips):
            self.copy("small0", place, place, self.small_s.at[k - 1], self.small_r.at[k - 1], dp=self.other_chip(k))

    def small_second(self):
        self.settle("small0")
        total = self.small_chip[0]
        for k in range(1, self.chips):
            total = total + self.small_chip[k]
        self.small_span[self.span] = total
        place = self.small_span.at[self.span]
        for k in range(1, self.spans):
            at = self.chips + k - 2
            self.copy("small1", place, place, self.small_s.at[at], self.small_r.at[at], span=self.other_span(k))

    def small_third(self):
        self.settle("small1")
        total = self.small_span[0]
        for k in range(1, self.spans):
            total = total + self.small_span[k]
        self.small_pair[self.core] = total
        place = self.small_pair.at[self.core]
        at = self.chips + self.spans - 2
        self.copy("small2", place, place, self.small_s.at[at], self.small_r.at[at], dp=self.partner())

    def small_last(self, out):
        self.settle("small2")
        half = self.small_pair.shape[2] - 128
        for c in range(2):
            out[:, pl.ds(c * half, half)] = self.small_pair[c, :, pl.ds(0, half)]
        out[:, pl.ds(2 * half, 128)] = self.small_pair[0, :, pl.ds(half, 128)] + self.small_pair[1, :, pl.ds(half, 128)]


def places_of(plan, half, depth, groups):
    room = [half] + [depth] * groups
    used = [0] * len(room)
    places = []
    for size, _ in plan:
        fits = [n for n in range(len(room)) if used[n] + size <= room[n]]
        if not fits:
            return None
        places.append((fits[0] - 1, used[fits[0]]))
        used[fits[0]] += size
    return places if used == room else None


def make_plan(half, depth, groups):
    if places_of(piece_plan, half, depth, groups):
        return piece_plan, piece_order
    count = (half + depth * groups) // half
    return ((half, "near"),) * count, tuple(range(count)) * 6


def reducer_scratch(pieces, rows, width, chips, spans, small_width):
    vmem, dma = pltpu.VMEM, pltpu.SemaphoreType.DMA
    return [
        vmem((pieces, rows, width), jnp.float32),
        vmem((pieces, rows, width), jnp.bfloat16),
        vmem((pieces, rows, width), jnp.bfloat16),
        vmem((pieces, max(rows, spans * rows // chips), width), jnp.bfloat16),
        vmem((chips, 1, small_width), jnp.float32),
        vmem((spans, 1, small_width), jnp.float32),
        vmem((2, 1, small_width), jnp.float32),
        dma((pieces,)), dma((pieces,)),
        dma((2, pieces, chips - 1)), dma((2, pieces, chips - 1)),
        dma((2, pieces, spans - 1)), dma((2, pieces, spans - 1)),
        dma((chips + spans - 1,)), dma((chips + spans - 1,)),
    ]


def write_kernel(first, second, small, first_out, second_out, bias_out, loss_out, first_buf, second_buf, bias_buf, loss_buf, sem):
    parts = first_buf.shape[0]
    rows = first_buf.shape[1]
    hid = bias_out.shape[1]
    bias_buf[...] = small[:, pl.ds(0, hid)]
    loss_buf[...] = small[:, pl.ds(hid, 1)]
    copies = [
        pltpu.make_async_copy(second_buf, second_out, sem.at[parts]),
        pltpu.make_async_copy(bias_buf, bias_out, sem.at[parts + 1]),
        pltpu.make_async_copy(loss_buf, loss_out, sem.at[parts + 2]),
    ]
    copies[1].start()
    copies[2].start()
    second_buf[...] = second[...].astype(jnp.float32)
    copies[0].start()
    for n in range(parts):
        at = pl.ds(n * rows, rows)
        for group in range(first.shape[0]):
            cols = pl.ds(group * first.shape[2], first.shape[2])
            first_buf[n, :, cols] = first[group, at, :].astype(jnp.float32)
        copies.append(pltpu.make_async_copy(first_buf.at[n], first_out.at[at], sem.at[n]))
        copies[-1].start()
    for copy in copies:
        copy.wait()


def dot(lhs, rhs, dims):
    return lax.dot_general(lhs, rhs, (dims, ((), ())), preferred_element_type=jnp.float32)


def ideal_gain(counts, list_len):
    places = (1 + lax.broadcasted_iota(jnp.int32, (1, list_len), 1)).astype(jnp.float32)
    discount = log_two / jnp.log(1.0 + places)
    total = jnp.zeros((1, 1), jnp.float32)
    start = jnp.zeros((1, 1), jnp.float32)
    for level in reversed(range(len(gain_values))):
        finish = start + counts[level : level + 1, 0:1]
        inside = (places > start) & (places <= finish)
        total = total + gain_values[level] * jnp.sum(jnp.where(inside, discount, 0.0), axis=1, keepdims=True)
        start = finish
    return jnp.maximum(total, 1.0)


def relay_keys(span, keys, send, recv):
    parts = 4
    size = keys.shape[1] // parts

    def made(n, src, dst, k):
        return pltpu.make_async_remote_copy(
            src_ref=src, dst_ref=dst, send_sem=send.at[n], recv_sem=recv.at[n],
            device_id={"dp": lax.axis_index("dp"), "span": other_of(span, k, 4)}, device_id_type=pl.DeviceIdType.MESH,
        )

    blocks = [pl.ds(n * size, size) for n in range(parts)]
    far = [made(n, keys.at[0, at], keys.at[2, at], 2) for n, at in enumerate(blocks)]
    passed = [made(parts + n, keys.at[2, at], keys.at[3, at], 1) for n, at in enumerate(blocks)]
    mid = made(2 * parts, keys.at[0], keys.at[3], 3)
    near = made(2 * parts + 1, keys.at[0], keys.at[1], 1)
    return far, mid, near, passed


def step_kernel(
    chips, spans, lengths, labels_hbm, features_hbm, w_first_hbm, b_first_hbm, w_second_hbm,
    first_out, second_out, small_out,
    labels, b_first, feats, w_first, w_second, feats_t, hidden_t, pre, pre_other, hidden, keys, embs, slopes, ranks,
    label_rows, grad_emb, grad_pre,
    load_sem, key_s, key_r, label_s, label_r, mate_s, mate_r, *scratch,
):
    dp, span = lax.axis_index("dp"), lax.axis_index("span")
    core, chip = lax.rem(dp, 2), dp // 2
    place = (core, chip, span)
    rows, depth = feats.shape[1:]
    width = w_second.shape[1]
    hid = w_first.shape[1]
    half = hid // 2
    half_width = width // 2
    pair_scale = 1.0 / math.sqrt(half_width)
    list_count, list_len = 2 * chips, rows * spans
    loads = [
        pltpu.make_async_copy(src, dst, load_sem.at[n])
        for n, (src, dst) in enumerate(
            (
                (features_hbm.at[0], feats.at[0]), (w_first_hbm, w_first), (w_second_hbm, w_second),
                (labels_hbm, labels), (b_first_hbm, b_first),
            )
        )
    ]
    for load in loads:
        load.start()
    enter = greet_peers(place, chips, spans)

    def to_spans(refs, send, recv):
        made = []
        for k in range(1, spans):
            copy = pltpu.make_async_remote_copy(
                src_ref=refs.at[0], dst_ref=refs.at[k], send_sem=send.at[k - 1], recv_sem=recv.at[k - 1],
                device_id={"dp": dp, "span": other_of(span, k, spans)}, device_id_type=pl.DeviceIdType.MESH,
            )
            copy.start()
            made.append(copy)
        return made

    def to_mate(n, src, dst):
        copy = pltpu.make_async_remote_copy(
            src_ref=src, dst_ref=dst, send_sem=mate_s.at[n], recv_sem=mate_r.at[n],
            device_id={"dp": dp + 1 - 2 * core, "span": span}, device_id_type=pl.DeviceIdType.MESH,
        )
        copy.start()
        return copy

    length = lengths[0]
    my_half = pl.ds(pl.multiple_of(core * half, half), half)

    def live_at(k, shape, dim):
        owner = owner_of(span, k, spans)
        return (owner * rows + lax.broadcasted_iota(jnp.int32, shape, dim) < length).astype(jnp.float32)

    def live_row(k):
        return live_at(k, (1, rows), 1)

    def live_col(k):
        return live_at(k, (rows, 1), 0)

    loads[3].wait()
    label_rows[0] = labels[...].astype(jnp.float32)
    loads[4].wait()
    loads[0].wait()
    loads[1].wait()
    for p in range(hid // width):
        cols = pl.ds(p * width, width)
        pre_act = dot(feats[0], w_first[:, cols], ((1,), (0,))) + b_first[:, cols]
        pre[:, cols] = pre_act
        hidden[:, cols] = jnp.maximum(pre_act, 0.0).astype(jnp.bfloat16)
    loads[2].wait()
    row_emb = dot(hidden[...], w_second[...], ((1,), (0,))).astype(jnp.bfloat16)
    keys[0] = jnp.concatenate([row_emb[:, half_width:], -row_emb[:, :half_width]], axis=1)
    enter()
    label_copies = to_spans(label_rows, label_s, label_r)
    if spans == 4:
        far_keys, mid_key, near_key, passed = relay_keys(span, keys, key_s, key_r)
        inner = lax.rem((span + 1) // 2, 2) == 1
        for copy in far_keys:
            copy.start()
        near_key.start()
        pl.when(inner)(mid_key.start)
    else:
        key_copies = to_spans(keys, key_s, key_r)
    feat_copy = to_mate(0, feats.at[0], feats.at[1])

    ranks[...] = jnp.zeros_like(ranks)

    def block(a, b, keep=False):
        above = jax.nn.sigmoid(dot(embs[a], keys[b], ((1,), (1,))) * pair_scale)
        ranks[b] += jnp.sum((above * live_col(a)).reshape(rows // 8, 8, rows), axis=0)
        if keep:
            slopes[b] = above * (1.0 - above)

    def meet(k):
        key_rows = keys[k]
        embs[k] = jnp.concatenate([-key_rows[:, half_width:], key_rows[:, :half_width]], axis=1)
        block(0, k, keep=True)
        if k:
            block(k, 0)
            block(k, k)

        def both(m, carry):
            block(m, k)
            block(k, m)
            return carry

        if k > 4:
            lax.fori_loop(1, k, both, 0)
        else:
            for m in range(1, k):
                both(m, 0)

    meet(0)
    feats_t[:, pl.ds(0, rows)] = feats[0].T
    hidden_t[:, pl.ds(0, rows)] = hidden[:, my_half].T
    feat_copy.wait()
    feats_t[:, pl.ds(rows, rows)] = feats[1].T
    other_act = dot(feats[1], w_first[:, my_half], ((1,), (0,))) + b_first[:, my_half]
    pre_other[...] = other_act
    hidden_t[:, pl.ds(rows, rows)] = jnp.maximum(other_act, 0.0).astype(jnp.bfloat16).T
    for copy in label_copies:
        copy.wait()
    levels = lax.broadcasted_iota(jnp.int32, (8, rows), 0).astype(jnp.float32)
    level_counts = jnp.zeros((8, 1), jnp.float32)
    for k in range(spans):
        level_counts = level_counts + jnp.sum(jnp.where(levels == label_rows[k], live_row(k), 0.0), axis=1, keepdims=True)
    ideal = ideal_gain(level_counts, list_len)
    if spans == 4:
        for copy, onward in zip(far_keys, passed):
            copy.wait_recv()
            pl.when(inner)(onward.start)
        near_key.wait_recv()
        meet(1)
        meet(2)
        pl.when(inner)(mid_key.wait)

        @pl.when(jnp.logical_not(inner))
        def _():
            for onward in passed:
                onward.wait_recv()

        meet(3)
    else:
        for k in range(1, spans):
            key_copies[k - 1].wait()
            meet(k)

    def rank_weight(k):
        gain = jnp.zeros((1, rows), jnp.float32)
        for level, value in enumerate(gain_values):
            gain = gain + jnp.where(label_rows[k] == level, value, 0.0)
        gain = gain * live_row(k)
        rank = 0.5 + jnp.sum(ranks[k], axis=0, keepdims=True)
        log_rank = jnp.log(1.0 + rank)
        weight = gain / (ideal * list_count) * log_two / ((1.0 + rank) * log_rank * log_rank)
        return weight, gain * log_two / log_rank

    eye = lax.broadcasted_iota(jnp.int32, (rows, rows), 0) == lax.broadcasted_iota(jnp.int32, (rows, rows), 1)
    own_weight, own_dcg = rank_weight(0)
    weight_col = jnp.sum(jnp.where(eye, own_weight, 0.0), axis=1, keepdims=True)
    own_live = live_col(0)
    total = jnp.zeros((rows, width), jnp.float32)
    for k in range(spans):
        weight = rank_weight(k)[0] if k else own_weight
        pair_grad = slopes[k] * (own_live * weight - weight_col * live_row(k))
        total = total + dot(pair_grad.astype(jnp.bfloat16), keys[k], ((1,), (0,)))
    grad_emb[0] = (total * pair_scale).astype(jnp.bfloat16)
    emb_copy = to_mate(1, grad_emb.at[0], grad_emb.at[1])
    if spans == 4:
        for copy in far_keys + [near_key]:
            copy.wait_send()

        @pl.when(inner)
        def _():
            for onward in passed:
                onward.wait_send()

    dcg = jnp.sum(own_dcg, axis=1, keepdims=True)
    loss_part = (1.0 / spans - dcg / ideal) / list_count

    def through(n, act):
        back = dot(grad_emb[n], w_second[my_half, :], ((1,), (1,)))
        grad_rows = jnp.where(act > 0.0, back, 0.0).astype(jnp.bfloat16)
        grad_pre[pl.ds(n * rows, rows), :] = grad_rows
        return jnp.sum(grad_rows.astype(jnp.float32), axis=0, keepdims=True)

    bias = through(0, pre[:, my_half])
    emb_copy.wait()

    plan, order = make_plan(half, depth, half // width)
    where = places_of(plan, half, depth, half // width)
    pieces = len(plan)

    def compute(p):
        group, start = where[p]
        rows = pl.ds(start, plan[p][0])
        if group < 0:
            return dot(hidden_t[rows, :], grad_emb[...].reshape(2 * feats.shape[1], width), ((1,), (0,)))
        return dot(feats_t[rows, :], grad_pre[:, pl.ds(group * width, width)], ((1,), (0,)))

    def result(p, side, start, size):
        group, base = where[p]
        if group < 0:
            return second_out.at[rows_at(side * half + base + start, size)]
        return first_out.at[side * (half // width) + group, rows_at(base + start, size)]

    red = Reducer(place, chips, spans, plan, compute, result, scratch)
    bias_after = min(p for p in range(pieces) if where[p][0] >= 0)
    smalls = {3 * pieces: red.small_second, 4 * pieces: red.small_third}
    for n, p in enumerate(order):
        if red.at[p] == 0 and p == bias_after:
            bias = bias + through(1, pre_other[...])
            red.small_first(jnp.concatenate([bias, jnp.broadcast_to(loss_part, (1, 128))], axis=1))
        red.advance(p)
        if n in smalls:
            smalls[n]()
    red.small_last(small_out)


def shards(features, lengths, labels, w_first, b_first, w_second):
    chips, spans = lax.axis_size("dp") // 2, lax.axis_size("span")
    rows, depth = features.shape[1:]
    hid, width = w_second.shape
    half = hid // 2
    plan, _ = make_plan(half, depth, half // width)
    pieces, piece_rows = len(plan), max(size for size, _ in plan)
    small_width = half + 128
    vmem, dma = pltpu.VMEM, pltpu.SemaphoreType.DMA
    in_vmem = pl.BlockSpec(memory_space=pltpu.VMEM)
    in_place = pl.BlockSpec(memory_space=pl.ANY)
    in_hbm = pl.BlockSpec(memory_space=pltpu.HBM)
    first_sum, second_sum, small_sum = pl.pallas_call(
        lambda *refs: step_kernel(chips, spans, *refs),
        name="rank_step",
        out_shape=(
            jax.ShapeDtypeStruct((hid // width, depth, width), jnp.bfloat16),
            jax.ShapeDtypeStruct((hid, width), jnp.bfloat16),
            jax.ShapeDtypeStruct((1, hid + 128), jnp.float32),
        ),
        in_specs=[pl.BlockSpec(memory_space=pltpu.SMEM)] + [in_hbm] * 5,
        out_specs=(in_vmem,) * 3,
        scratch_shapes=[
            vmem((1, rows), jnp.int32),
            vmem((1, hid), jnp.float32),
            vmem((2, rows, depth), jnp.bfloat16),
            vmem((depth, hid), jnp.bfloat16),
            vmem((hid, width), jnp.bfloat16),
            vmem((depth, 2 * rows), jnp.bfloat16),
            vmem((half, 2 * rows), jnp.bfloat16),
            vmem((rows, hid), jnp.float32),
            vmem((rows, half), jnp.float32),
            vmem((rows, hid), jnp.bfloat16),
            vmem((spans, rows, width), jnp.bfloat16),
            vmem((spans, rows, width), jnp.bfloat16),
            vmem((spans, rows, rows), jnp.float32),
            vmem((spans, 8, rows), jnp.float32),
            vmem((spans, 1, rows), jnp.float32),
            vmem((2, rows, width), jnp.bfloat16),
            vmem((2 * rows, half), jnp.bfloat16),
            dma((5,)),
            dma((spans + 9,)), dma((spans + 9,)), dma((spans - 1,)), dma((spans - 1,)),
            dma((2,)), dma((2,)),
        ]
        + reducer_scratch(pieces, piece_rows, width, chips, spans, small_width),
        compiler_params=pltpu.CompilerParams(collective_id=0, has_side_effects=True, vmem_limit_bytes=40 << 20),
    )(lengths, *(pltpu.with_memory_space_constraint(x, pltpu.HBM) for x in (labels, features, w_first, b_first.reshape(1, -1), w_second)))
    parts = 4
    first, second, bias, loss = pl.pallas_call(
        write_kernel,
        name="write_out",
        out_shape=(
            jax.ShapeDtypeStruct((depth, hid), jnp.float32),
            jax.ShapeDtypeStruct((hid, width), jnp.float32),
            jax.ShapeDtypeStruct((1, hid), jnp.float32),
            jax.ShapeDtypeStruct((1, 1), jnp.float32),
        ),
        in_specs=[in_vmem] * 3,
        out_specs=(in_place,) * 4,
        scratch_shapes=[
            vmem((parts, depth // parts, hid), jnp.float32),
            vmem((hid, width), jnp.float32),
            vmem((1, hid), jnp.float32),
            vmem((1, 1), jnp.float32),
            dma((parts + 3,)),
        ],
        compiler_params=pltpu.CompilerParams(vmem_limit_bytes=16 << 20),
    )(first_sum, second_sum, small_sum)
    return loss[0, 0], first, bias[0], second


def solution(mesh):
    placed = (P("dp", "span", None), P("dp"), P("dp", "span"), P(), P(), P())
    return jax.shard_map(
        shards, mesh=mesh, in_specs=placed, out_specs=(P(), P(), P(), P()), check_vma=False
    )
```

```python
import math

import jax
import jax.numpy as jnp
from jax import lax
from jax.experimental import pallas as pl
from jax.experimental.pallas import tpu as pltpu
from jax.sharding import PartitionSpec as P

gain_values = (0.0, 1.0, 3.0, 7.0, 15.0)
log_two = math.log(2.0)
piece_plan = ((512, "near"), (512, "far"), (512, "near"), (512, "near"), (256, "near"), (256, "near"))
piece_order = (
    0, 1, 2, 3, 0, 2, 4, 1, 0, 5, 3, 2, 4, 1, 5, 0, 3, 2, 4, 5,
    1, 3, 0, 5, 4, 0, 3, 2, 1, 5, 3, 4, 1, 5, 2, 4,
)


def greet_peers(place, chips, spans):
    core, chip, span = place
    barrier = pltpu.get_barrier_semaphore()
    peers = [{"dp": 2 * chip + 1 - core, "span": span}]
    peers += [{"dp": 2 * other_of(chip, k, chips) + core, "span": span} for k in range(1, chips)]
    peers += [{"dp": 2 * chip + core, "span": other_of(span, k, spans)} for k in range(1, spans)]
    for peer in peers:
        pl.semaphore_signal(barrier, inc=1, device_id=peer, device_id_type=pl.DeviceIdType.MESH)
    return lambda: pl.semaphore_wait(barrier, len(peers))


def other_of(me, k, count):
    if count & (count - 1):
        return lax.rem(me + k, count)
    bits = [1 << n for n in range(count.bit_length() - 1)]
    return me + sum((1 - 2 * lax.rem(me // bit, 2)) * (k // bit % 2 * bit) for bit in bits)


def owner_of(me, k, count):
    if count & (count - 1):
        return lax.rem(me - k + count, count)
    return other_of(me, k, count)


def rows_at(start, size):
    return pl.ds(pl.multiple_of(start, size), size)


def owners_of(rows, chips, spans):
    return min(spans, rows // chips // 16)


class Reducer:
    def __init__(self, place, chips, spans, plan, compute, result, scratch):
        self.core, self.chip, self.span = place
        self.chips, self.spans = chips, spans
        self.compute, self.result = compute, result
        (
            self.full_sum, self.buf, self.chip_in, self.span_in,
            self.small_chip, self.small_span, self.small_pair,
            self.pair_s, self.pair_r, self.chip_s, self.chip_r, self.span_s, self.span_r,
            self.small_s, self.small_r,
        ) = scratch
        self.rows = [size for size, _ in plan]
        self.block = [size // chips for size in self.rows]
        self.owners = [owners_of(size, chips, spans) for size in self.rows]
        self.part = [block // owners for block, owners in zip(self.block, self.owners)]
        self.copies = {}
        self.chip_steps = sorted(range(1, chips), key=lambda k: (-bin(k).count("1"), -k))
        far = [size // spans // chips >= 16 for size in self.rows]
        near = (self.near_out, self.near_span, self.near_back, self.near_chip, self.pair_back, self.last)
        every = (self.near_out, self.every_span, self.every_chip, self.pair_back, self.last)
        remote = (self.far_out, self.far_chip, self.far_back, self.far_span, self.pair_back, self.last)
        self.stages = [{"near": near, "every": every, "far": remote if far[p] else near}[kind] for p, (_, kind) in enumerate(plan)]
        self.at = [0] * len(plan)

    def advance(self, p):
        self.stages[p][self.at[p]](p)
        self.at[p] += 1

    def copy(self, key, src, dst, send, recv, dp=None, span=None):
        peer = {
            "dp": 2 * self.chip + self.core if dp is None else dp,
            "span": self.span if span is None else span,
        }
        made = pltpu.make_async_remote_copy(
            src_ref=src, dst_ref=dst, send_sem=send, recv_sem=recv,
            device_id=peer, device_id_type=pl.DeviceIdType.MESH,
        )
        made.start()
        self.copies.setdefault(key, []).append(made)

    def to_chip(self, p, n, k, src, dst):
        self.copy(p, src, dst, self.chip_s.at[n, p, k - 1], self.chip_r.at[n, p, k - 1], dp=self.other_chip(k))

    def to_span(self, p, n, k, src, dst):
        self.copy(p, src, dst, self.span_s.at[n, p, k - 1], self.span_r.at[n, p, k - 1], span=self.other_span(k))

    def settle(self, key):
        for made in self.copies.pop(key, []):
            made.wait()

    def partner(self):
        return 2 * self.chip + 1 - self.core

    def other_chip(self, k):
        return 2 * other_of(self.chip, k, self.chips) + self.core

    def other_span(self, k):
        return other_of(self.span, k, self.spans)

    def begin(self, p):
        total = self.compute(p)
        rows = pl.ds(0, self.rows[p])
        self.full_sum[p, rows] = total
        self.buf[p, rows] = total.astype(jnp.bfloat16)

    def gathered(self, p, mine, arrived, count, size):
        self.settle(p)
        total = self.full_sum[p, mine]
        for k in range(count):
            total = total + arrived[p, pl.ds(k * size, size)].astype(jnp.float32)
        return total

    def spread_chips(self, p, base):
        for k in self.chip_steps:
            rows = rows_at(base + other_of(self.chip, k, self.chips) * self.block[p], self.block[p])
            self.to_chip(p, 0, k, self.buf.at[p, rows], self.chip_in.at[p, pl.ds((k - 1) * self.block[p], self.block[p])])

    def near_out(self, p):
        self.begin(p)
        self.spread_chips(p, 0)

    def near_sum(self, p):
        return self.gathered(p, rows_at(self.chip * self.block[p], self.block[p]), self.chip_in, self.chips - 1, self.block[p])

    def near_span(self, p):
        total = self.near_sum(p)
        mine = rows_at(self.chip * self.block[p], self.block[p])
        self.full_sum[p, mine] = total
        self.buf[p, mine] = total.astype(jnp.bfloat16)
        for k in range(1, self.spans):
            to = self.other_span(k)
            rows = rows_at(self.chip * self.block[p] + lax.rem(to, self.owners[p]) * self.part[p], self.part[p])
            self.to_span(p, 0, k, self.buf.at[p, rows], self.span_in.at[p, pl.ds((k - 1) * self.part[p], self.part[p])])

    def near_back(self, p):
        mine = lax.rem(self.span, self.owners[p])
        start = self.chip * self.block[p] + mine * self.part[p]
        rows = rows_at(start, self.part[p])
        if self.owners[p] < self.spans:
            self.full_sum[p, rows] = self.buf[p, rows].astype(jnp.float32)
        total = self.gathered(p, rows, self.span_in, self.spans - 1, self.part[p])
        place = self.result(p, self.core, start, self.part[p])
        place[...] = total.astype(jnp.bfloat16)
        for k in range(1, self.owners[p]):
            to = self.span - mine + other_of(mine, k, self.owners[p])
            self.copy(p, place, place, self.span_s.at[1, p, k - 1], self.span_r.at[1, p, k - 1], span=to)

    def back_chips(self, p, start):
        place = self.result(p, self.core, start, self.block[p])
        for k in self.chip_steps:
            self.to_chip(p, 1, k, place, place)

    def near_chip(self, p):
        self.settle(p)
        self.back_chips(p, self.chip * self.block[p])

    def every_span(self, p):
        slot = self.span_in.at[p, rows_at(self.span * self.block[p], self.block[p])]
        slot[...] = self.near_sum(p).astype(jnp.bfloat16)
        for k in range(1, self.spans):
            self.to_span(p, 0, k, slot, slot)

    def every_chip(self, p):
        self.settle(p)
        total = self.span_in[p, pl.ds(0, self.block[p])].astype(jnp.float32)
        for k in range(1, self.spans):
            total = total + self.span_in[p, pl.ds(k * self.block[p], self.block[p])].astype(jnp.float32)
        self.result(p, self.core, self.chip * self.block[p], self.block[p])[...] = total.astype(jnp.bfloat16)
        self.back_chips(p, self.chip * self.block[p])

    def far_out(self, p):
        self.begin(p)
        size = self.rows[p] // self.spans
        for k in range(1, self.spans):
            rows = rows_at(self.other_span(k) * size, size)
            self.to_span(p, 0, k, self.buf.at[p, rows], self.span_in.at[p, pl.ds((k - 1) * size, size)])

    def far_chip(self, p):
        size = self.rows[p] // self.spans
        mine = rows_at(self.span * size, size)
        total = self.gathered(p, mine, self.span_in, self.spans - 1, size)
        self.full_sum[p, mine] = total
        self.buf[p, mine] = total.astype(jnp.bfloat16)
        small = size // self.chips
        for k in self.chip_steps:
            rows = rows_at(self.span * size + other_of(self.chip, k, self.chips) * small, small)
            self.to_chip(p, 0, k, self.buf.at[p, rows], self.chip_in.at[p, pl.ds((k - 1) * small, small)])

    def far_back(self, p):
        size = self.rows[p] // self.spans
        small = size // self.chips
        start = self.span * size + self.chip * small
        total = self.gathered(p, rows_at(start, small), self.chip_in, self.chips - 1, small)
        place = self.result(p, self.core, start, small)
        place[...] = total.astype(jnp.bfloat16)
        for k in self.chip_steps:
            self.to_chip(p, 1, k, place, place)

    def far_span(self, p):
        self.settle(p)
        size = self.rows[p] // self.spans
        place = self.result(p, self.core, self.span * size, size)
        for k in range(1, self.spans):
            self.to_span(p, 1, k, place, place)

    def pair_back(self, p):
        self.settle(p)
        place = self.result(p, self.core, 0, self.rows[p])
        self.copy(p, place, place, self.pair_s.at[p], self.pair_r.at[p], dp=self.partner())

    def last(self, p):
        self.settle(p)

    def small_first(self, values):
        self.small_chip[self.chip] = values
        place = self.small_chip.at[self.chip]
        for k in range(1, self.chips):
            self.copy("small0", place, place, self.small_s.at[k - 1], self.small_r.at[k - 1], dp=self.other_chip(k))

    def small_second(self):
        self.settle("small0")
        total = self.small_chip[0]
        for k in range(1, self.chips):
            total = total + self.small_chip[k]
        self.small_span[self.span] = total
        place = self.small_span.at[self.span]
        for k in range(1, self.spans):
            at = self.chips + k - 2
            self.copy("small1", place, place, self.small_s.at[at], self.small_r.at[at], span=self.other_span(k))

    def small_third(self):
        self.settle("small1")
        total = self.small_span[0]
        for k in range(1, self.spans):
            total = total + self.small_span[k]
        self.small_pair[self.core] = total
        place = self.small_pair.at[self.core]
        at = self.chips + self.spans - 2
        self.copy("small2", place, place, self.small_s.at[at], self.small_r.at[at], dp=self.partner())

    def small_last(self, out):
        self.settle("small2")
        half = self.small_pair.shape[2] - 128
        for c in range(2):
            out[:, pl.ds(c * half, half)] = self.small_pair[c, :, pl.ds(0, half)]
        out[:, pl.ds(2 * half, 128)] = self.small_pair[0, :, pl.ds(half, 128)] + self.small_pair[1, :, pl.ds(half, 128)]


def places_of(plan, half, depth, groups):
    room = [half] + [depth] * groups
    used = [0] * len(room)
    places = []
    for size, _ in plan:
        fits = [n for n in range(len(room)) if used[n] + size <= room[n]]
        if not fits:
            return None
        places.append((fits[0] - 1, used[fits[0]]))
        used[fits[0]] += size
    return places if used == room else None


def make_plan(half, depth, groups):
    if places_of(piece_plan, half, depth, groups):
        return piece_plan, piece_order
    count = (half + depth * groups) // half
    return ((half, "near"),) * count, tuple(range(count)) * 6


def reducer_scratch(pieces, rows, width, chips, spans, small_width):
    vmem, dma = pltpu.VMEM, pltpu.SemaphoreType.DMA
    return [
        vmem((pieces, rows, width), jnp.float32),
        vmem((pieces, rows, width), jnp.bfloat16),
        vmem((pieces, rows, width), jnp.bfloat16),
        vmem((pieces, max(rows, spans * rows // chips), width), jnp.bfloat16),
        vmem((chips, 1, small_width), jnp.float32),
        vmem((spans, 1, small_width), jnp.float32),
        vmem((2, 1, small_width), jnp.float32),
        dma((pieces,)), dma((pieces,)),
        dma((2, pieces, chips - 1)), dma((2, pieces, chips - 1)),
        dma((2, pieces, spans - 1)), dma((2, pieces, spans - 1)),
        dma((chips + spans - 1,)), dma((chips + spans - 1,)),
    ]


def write_kernel(first, second, small, first_out, second_out, bias_out, loss_out, first_buf, second_buf, bias_buf, loss_buf, sem):
    parts = first_buf.shape[0]
    rows = first_buf.shape[1]
    hid = bias_out.shape[1]
    bias_buf[...] = small[:, pl.ds(0, hid)]
    loss_buf[...] = small[:, pl.ds(hid, 1)]
    copies = [
        pltpu.make_async_copy(second_buf, second_out, sem.at[parts]),
        pltpu.make_async_copy(bias_buf, bias_out, sem.at[parts + 1]),
        pltpu.make_async_copy(loss_buf, loss_out, sem.at[parts + 2]),
    ]
    copies[1].start()
    copies[2].start()
    second_buf[...] = second[...].astype(jnp.float32)
    copies[0].start()
    for n in range(parts):
        at = pl.ds(n * rows, rows)
        for group in range(first.shape[0]):
            cols = pl.ds(group * first.shape[2], first.shape[2])
            first_buf[n, :, cols] = first[group, at, :].astype(jnp.float32)
        copies.append(pltpu.make_async_copy(first_buf.at[n], first_out.at[at], sem.at[n]))
        copies[-1].start()
    for copy in copies:
        copy.wait()


def dot(lhs, rhs, dims):
    return lax.dot_general(lhs, rhs, (dims, ((), ())), preferred_element_type=jnp.float32)


def ideal_gain(counts, list_len):
    places = (1 + lax.broadcasted_iota(jnp.int32, (1, list_len), 1)).astype(jnp.float32)
    discount = log_two / jnp.log(1.0 + places)
    total = jnp.zeros((1, 1), jnp.float32)
    start = jnp.zeros((1, 1), jnp.float32)
    for level in reversed(range(len(gain_values))):
        finish = start + counts[level : level + 1, 0:1]
        inside = (places > start) & (places <= finish)
        total = total + gain_values[level] * jnp.sum(jnp.where(inside, discount, 0.0), axis=1, keepdims=True)
        start = finish
    return jnp.maximum(total, 1.0)


def relay_keys(span, keys, send, recv):
    parts = 4
    size = keys.shape[1] // parts

    def made(n, src, dst, k):
        return pltpu.make_async_remote_copy(
            src_ref=src, dst_ref=dst, send_sem=send.at[n], recv_sem=recv.at[n],
            device_id={"dp": lax.axis_index("dp"), "span": other_of(span, k, 4)}, device_id_type=pl.DeviceIdType.MESH,
        )

    blocks = [pl.ds(n * size, size) for n in range(parts)]
    far = [made(n, keys.at[0, at], keys.at[2, at], 2) for n, at in enumerate(blocks)]
    passed = [made(parts + n, keys.at[2, at], keys.at[3, at], 1) for n, at in enumerate(blocks)]
    mid = made(2 * parts, keys.at[0], keys.at[3], 3)
    near = made(2 * parts + 1, keys.at[0], keys.at[1], 1)
    return far, mid, near, passed


def step_kernel(
    chips, spans, lengths, labels_hbm, features_hbm, w_first_hbm, b_first_hbm, w_second_hbm,
    first_out, second_out, small_out,
    labels, b_first, feats, w_first, w_second, feats_t, hidden_t, pre, pre_other, hidden, keys, embs, slopes, ranks,
    label_rows, grad_emb, grad_pre,
    load_sem, key_s, key_r, label_s, label_r, mate_s, mate_r, *scratch,
):
    dp, span = lax.axis_index("dp"), lax.axis_index("span")
    core, chip = lax.rem(dp, 2), dp // 2
    place = (core, chip, span)
    rows, depth = feats.shape[1:]
    width = w_second.shape[1]
    hid = w_first.shape[1]
    half = hid // 2
    half_width = width // 2
    pair_scale = 1.0 / math.sqrt(half_width)
    list_count, list_len = 2 * chips, rows * spans
    loads = [
        pltpu.make_async_copy(src, dst, load_sem.at[n])
        for n, (src, dst) in enumerate(
            (
                (features_hbm.at[0], feats.at[0]), (w_first_hbm, w_first), (w_second_hbm, w_second),
                (labels_hbm, labels), (b_first_hbm, b_first),
            )
        )
    ]
    for load in loads:
        load.start()
    enter = greet_peers(place, chips, spans)

    def to_spans(refs, send, recv):
        made = []
        for k in range(1, spans):
            copy = pltpu.make_async_remote_copy(
                src_ref=refs.at[0], dst_ref=refs.at[k], send_sem=send.at[k - 1], recv_sem=recv.at[k - 1],
                device_id={"dp": dp, "span": other_of(span, k, spans)}, device_id_type=pl.DeviceIdType.MESH,
            )
            copy.start()
            made.append(copy)
        return made

    def to_mate(n, src, dst):
        copy = pltpu.make_async_remote_copy(
            src_ref=src, dst_ref=dst, send_sem=mate_s.at[n], recv_sem=mate_r.at[n],
            device_id={"dp": dp + 1 - 2 * core, "span": span}, device_id_type=pl.DeviceIdType.MESH,
        )
        copy.start()
        return copy

    length = lengths[0]
    my_half = pl.ds(pl.multiple_of(core * half, half), half)

    def live_at(k, shape, dim):
        owner = owner_of(span, k, spans)
        return (owner * rows + lax.broadcasted_iota(jnp.int32, shape, dim) < length).astype(jnp.float32)

    def live_row(k):
        return live_at(k, (1, rows), 1)

    def live_col(k):
        return live_at(k, (rows, 1), 0)

    loads[3].wait()
    label_rows[0] = labels[...].astype(jnp.float32)
    loads[4].wait()
    loads[0].wait()
    loads[1].wait()
    for p in range(hid // width):
        cols = pl.ds(p * width, width)
        pre_act = dot(feats[0], w_first[:, cols], ((1,), (0,))) + b_first[:, cols]
        pre[:, cols] = pre_act
        hidden[:, cols] = jnp.maximum(pre_act, 0.0).astype(jnp.bfloat16)
    loads[2].wait()
    row_emb = dot(hidden[...], w_second[...], ((1,), (0,))).astype(jnp.bfloat16)
    keys[0] = jnp.concatenate([row_emb[:, half_width:], -row_emb[:, :half_width]], axis=1)
    enter()
    label_copies = to_spans(label_rows, label_s, label_r)
    if spans == 4:
        far_keys, mid_key, near_key, passed = relay_keys(span, keys, key_s, key_r)
        inner = lax.rem((span + 1) // 2, 2) == 1
        for copy in far_keys:
            copy.start()
        near_key.start()
        pl.when(inner)(mid_key.start)
    else:
        key_copies = to_spans(keys, key_s, key_r)
    feat_copy = to_mate(0, feats.at[0], feats.at[1])

    ranks[...] = jnp.zeros_like(ranks)

    def block(a, b, keep=False):
        above = jax.nn.sigmoid(dot(embs[a], keys[b], ((1,), (1,))) * pair_scale)
        ranks[b] += jnp.sum((above * live_col(a)).reshape(rows // 8, 8, rows), axis=0)
        if keep:
            slopes[b] = above * (1.0 - above)

    def meet(k):
        key_rows = keys[k]
        embs[k] = jnp.concatenate([-key_rows[:, half_width:], key_rows[:, :half_width]], axis=1)
        block(0, k, keep=True)
        if k:
            block(k, 0)
            block(k, k)

        def both(m, carry):
            block(m, k)
            block(k, m)
            return carry

        if k > 4:
            lax.fori_loop(1, k, both, 0)
        else:
            for m in range(1, k):
                both(m, 0)

    meet(0)
    feats_t[:, pl.ds(0, rows)] = feats[0].T
    hidden_t[:, pl.ds(0, rows)] = hidden[:, my_half].T
    feat_copy.wait()
    feats_t[:, pl.ds(rows, rows)] = feats[1].T
    other_act = dot(feats[1], w_first[:, my_half], ((1,), (0,))) + b_first[:, my_half]
    pre_other[...] = other_act
    hidden_t[:, pl.ds(rows, rows)] = jnp.maximum(other_act, 0.0).astype(jnp.bfloat16).T
    for copy in label_copies:
        copy.wait()
    levels = lax.broadcasted_iota(jnp.int32, (8, rows), 0).astype(jnp.float32)
    level_counts = jnp.zeros((8, 1), jnp.float32)
    for k in range(spans):
        level_counts = level_counts + jnp.sum(jnp.where(levels == label_rows[k], live_row(k), 0.0), axis=1, keepdims=True)
    ideal = ideal_gain(level_counts, list_len)
    if spans == 4:
        for copy, onward in zip(far_keys, passed):
            copy.wait_recv()
            pl.when(inner)(onward.start)
        near_key.wait_recv()
        meet(1)
        meet(2)
        pl.when(inner)(mid_key.wait)

        @pl.when(jnp.logical_not(inner))
        def _():
            for onward in passed:
                onward.wait_recv()

        meet(3)
    else:
        for k in range(1, spans):
            key_copies[k - 1].wait()
            meet(k)

    def rank_weight(k):
        gain = jnp.zeros((1, rows), jnp.float32)
        for level, value in enumerate(gain_values):
            gain = gain + jnp.where(label_rows[k] == level, value, 0.0)
        gain = gain * live_row(k)
        rank = 0.5 + jnp.sum(ranks[k], axis=0, keepdims=True)
        log_rank = jnp.log(1.0 + rank)
        weight = gain / (ideal * list_count) * log_two / ((1.0 + rank) * log_rank * log_rank)
        return weight, gain * log_two / log_rank

    eye = lax.broadcasted_iota(jnp.int32, (rows, rows), 0) == lax.broadcasted_iota(jnp.int32, (rows, rows), 1)
    own_weight, own_dcg = rank_weight(0)
    weight_col = jnp.sum(jnp.where(eye, own_weight, 0.0), axis=1, keepdims=True)
    own_live = live_col(0)
    total = jnp.zeros((rows, width), jnp.float32)
    for k in range(spans):
        weight = rank_weight(k)[0] if k else own_weight
        pair_grad = slopes[k] * (own_live * weight - weight_col * live_row(k))
        total = total + dot(pair_grad.astype(jnp.bfloat16), keys[k], ((1,), (0,)))
    grad_emb[0] = (total * pair_scale).astype(jnp.bfloat16)
    emb_copy = to_mate(1, grad_emb.at[0], grad_emb.at[1])
    if spans == 4:
        for copy in far_keys + [near_key]:
            copy.wait_send()

        @pl.when(inner)
        def _():
            for onward in passed:
                onward.wait_send()

    dcg = jnp.sum(own_dcg, axis=1, keepdims=True)
    loss_part = (1.0 / spans - dcg / ideal) / list_count

    def through(n, act):
        back = dot(grad_emb[n], w_second[my_half, :], ((1,), (1,)))
        grad_rows = jnp.where(act > 0.0, back, 0.0).astype(jnp.bfloat16)
        grad_pre[pl.ds(n * rows, rows), :] = grad_rows
        return jnp.sum(grad_rows.astype(jnp.float32), axis=0, keepdims=True)

    bias = through(0, pre[:, my_half])
    emb_copy.wait()

    plan, order = make_plan(half, depth, half // width)
    where = places_of(plan, half, depth, half // width)
    pieces = len(plan)

    def compute(p):
        group, start = where[p]
        rows = pl.ds(start, plan[p][0])
        if group < 0:
            return dot(hidden_t[rows, :], grad_emb[...].reshape(2 * feats.shape[1], width), ((1,), (0,)))
        return dot(feats_t[rows, :], grad_pre[:, pl.ds(group * width, width)], ((1,), (0,)))

    def result(p, side, start, size):
        group, base = where[p]
        if group < 0:
            return second_out.at[rows_at(side * half + base + start, size)]
        return first_out.at[side * (half // width) + group, rows_at(base + start, size)]

    red = Reducer(place, chips, spans, plan, compute, result, scratch)
    bias_after = min(p for p in range(pieces) if where[p][0] >= 0)
    smalls = {2 * pieces: red.small_second, 3 * pieces: red.small_third}
    for n, p in enumerate(order):
        if red.at[p] == 0 and p == bias_after:
            bias = bias + through(1, pre_other[...])
            red.small_first(jnp.concatenate([bias, jnp.broadcast_to(loss_part, (1, 128))], axis=1))
        red.advance(p)
        if n in smalls:
            smalls[n]()
    red.small_last(small_out)


def shards(features, lengths, labels, w_first, b_first, w_second):
    chips, spans = lax.axis_size("dp") // 2, lax.axis_size("span")
    rows, depth = features.shape[1:]
    hid, width = w_second.shape
    half = hid // 2
    plan, _ = make_plan(half, depth, half // width)
    pieces, piece_rows = len(plan), max(size for size, _ in plan)
    small_width = half + 128
    vmem, dma = pltpu.VMEM, pltpu.SemaphoreType.DMA
    in_vmem = pl.BlockSpec(memory_space=pltpu.VMEM)
    in_place = pl.BlockSpec(memory_space=pl.ANY)
    in_hbm = pl.BlockSpec(memory_space=pltpu.HBM)
    first_sum, second_sum, small_sum = pl.pallas_call(
        lambda *refs: step_kernel(chips, spans, *refs),
        name="rank_step",
        out_shape=(
            jax.ShapeDtypeStruct((hid // width, depth, width), jnp.bfloat16),
            jax.ShapeDtypeStruct((hid, width), jnp.bfloat16),
            jax.ShapeDtypeStruct((1, hid + 128), jnp.float32),
        ),
        in_specs=[pl.BlockSpec(memory_space=pltpu.SMEM)] + [in_hbm] * 5,
        out_specs=(in_vmem,) * 3,
        scratch_shapes=[
            vmem((1, rows), jnp.int32),
            vmem((1, hid), jnp.float32),
            vmem((2, rows, depth), jnp.bfloat16),
            vmem((depth, hid), jnp.bfloat16),
            vmem((hid, width), jnp.bfloat16),
            vmem((depth, 2 * rows), jnp.bfloat16),
            vmem((half, 2 * rows), jnp.bfloat16),
            vmem((rows, hid), jnp.float32),
            vmem((rows, half), jnp.float32),
            vmem((rows, hid), jnp.bfloat16),
            vmem((spans, rows, width), jnp.bfloat16),
            vmem((spans, rows, width), jnp.bfloat16),
            vmem((spans, rows, rows), jnp.float32),
            vmem((spans, 8, rows), jnp.float32),
            vmem((spans, 1, rows), jnp.float32),
            vmem((2, rows, width), jnp.bfloat16),
            vmem((2 * rows, half), jnp.bfloat16),
            dma((5,)),
            dma((spans + 9,)), dma((spans + 9,)), dma((spans - 1,)), dma((spans - 1,)),
            dma((2,)), dma((2,)),
        ]
        + reducer_scratch(pieces, piece_rows, width, chips, spans, small_width),
        compiler_params=pltpu.CompilerParams(collective_id=0, has_side_effects=True, vmem_limit_bytes=40 << 20),
    )(lengths, *(pltpu.with_memory_space_constraint(x, pltpu.HBM) for x in (labels, features, w_first, b_first.reshape(1, -1), w_second)))
    parts = 4
    first, second, bias, loss = pl.pallas_call(
        write_kernel,
        name="write_out",
        out_shape=(
            jax.ShapeDtypeStruct((depth, hid), jnp.float32),
            jax.ShapeDtypeStruct((hid, width), jnp.float32),
            jax.ShapeDtypeStruct((1, hid), jnp.float32),
            jax.ShapeDtypeStruct((1, 1), jnp.float32),
        ),
        in_specs=[in_vmem] * 3,
        out_specs=(in_place,) * 4,
        scratch_shapes=[
            vmem((parts, depth // parts, hid), jnp.float32),
            vmem((hid, width), jnp.float32),
            vmem((1, hid), jnp.float32),
            vmem((1, 1), jnp.float32),
            dma((parts + 3,)),
        ],
        compiler_params=pltpu.CompilerParams(vmem_limit_bytes=16 << 20),
    )(first_sum, second_sum, small_sum)
    return loss[0, 0], first, bias[0], second


def solution(mesh):
    placed = (P("dp", "span", None), P("dp"), P("dp", "span"), P(), P(), P())
    return jax.shard_map(
        shards, mesh=mesh, in_specs=placed, out_specs=(P(), P(), P(), P()), check_vma=False
    )
```
